32 devices in a mesh: ta: 2 (over y), ha: 4 (over z), wa: 4 (over x, core).
Axes of the slice: x: 2, y: 2, z: 4, core: 2. Of those that a mesh axis runs over, the one named last changes fastest.
Arguments:
- latents: bfloat16 [1, 8, 32, 32, 3072], P(None, 'ta', 'ha', 'wa'), may hold values from -6 to 6
- input_weight: bfloat16 [3072, 3, 16, 128], P(None, None, 'ta'), as said below
- norm_gains: float32 [2, 128], replicated, may hold values from 0.6 to 5
- output_weight: bfloat16 [16, 128, 3072], P('ta'), may hold values from -0.125 to 0.125
Outputs:
- mixed: bfloat16 [1, 8, 32, 32, 3072], P(None, 'ta', 'ha', 'wa')
The draws below stay inside these ranges and needn't reach their ends.
Inputs may be any that keep to these rules, and one draw needn't show every extreme that they name: `input_weight`: every entry has magnitude at most 6.3 / sqrt(3072).
All inputs are finite; a program needn't handle non-finite values.
Results may differ from the reference program's by a relative error of at most 0.0077.
Values may be sent and summed in bfloat16 or wider, within the bound.
No kernel may reach another device: no remote copies, remote signals or barrier semaphores. Data moves between devices by JAX's collectives and lax.ppermute only.
A program may use at most 320 MiB of HBM per device.

```python
import math
import jax
import jax.numpy as jnp
from jax import lax

D = 3072
HEADS = 16
HD = 128
TILE_T = 4
TILE_S = 8
FRAMES = 8
CLIPS = 1
HEIGHT = 32
WIDTH = 32


def draw_input_weight(key, part):
    base_key = jax.random.fold_in(key, 11)
    spread = D ** (-0.5)
    drawn_part = jax.random.truncated_normal(base_key, -6.0, 6.0, (D, 3, HEADS, HD), jnp.float32) * spread
    weights = drawn_part
    return weights.astype(jnp.bfloat16)


def draw_norm_gains(key, part):
    gain_key = jax.random.fold_in(key, 37)
    gains_drawn = jax.random.uniform(gain_key, (2, HD), jnp.float32, 0.6, 1.6)
    return gains_drawn


def shard_levels(stream_key, shape, cuts, smallest, top_value):
    level, own = 1.0, jax.random.fold_in(stream_key, 6)
    for axis_at, parts in cuts:
        steps = jnp.exp(jax.random.uniform(jax.random.fold_in(own, axis_at), (parts,), jnp.float32, smallest / len(cuts), top_value / len(cuts)))
        level = level * jnp.repeat(steps, shape[axis_at] // parts).reshape([-1 if axis == axis_at else 1 for axis in range(len(shape))])
    return level


def normal_values(key, extent, scale, most, pieces=(), held_as=jnp.bfloat16):
    result = jax.random.normal(key, extent, jnp.float32) * scale
    if len(pieces) > 0:
        result = shard_levels(key, extent, pieces, -0.22, 0.18) * result
    return jnp.clip(result, min=-most, max=most).astype(held_as)


def setup_inputs(seed: int = 0) -> dict:
    arg_keys = jax.random.split(jax.random.key(seed), 5)
    return {
        "latents": normal_values(arg_keys[0], (CLIPS, FRAMES, HEIGHT, WIDTH, D), 1.0, 6.0, ((1, 2), (2, 4), (3, 4))),
        "input_weight": draw_input_weight(jax.random.fold_in(arg_keys[4], 71), 0),
        "norm_gains": draw_norm_gains(jax.random.fold_in(arg_keys[4], 71), 0),
        "output_weight": normal_values(arg_keys[3], (HEADS, HD, D), (HEADS * HD) ** -0.5, 0.125, ((0, 2),)),
    }


EPSILON = 1e-06

def rms_norm(values, gain_row):
    mean_square = lax.optimization_barrier(jnp.mean(values * values, axis=-1, keepdims=True))
    return values * lax.rsqrt(mean_square + EPSILON) * gain_row

def to_tiles(array, tiles_high, tiles_wide):
    shaped = array.reshape(CLIPS, FRAMES, tiles_high, TILE_S, tiles_wide, TILE_S, HEADS, HD)
    shaped = shaped.transpose(2, 4, 0, 6, 1, 3, 5, 7)
    return shaped.reshape(tiles_high, tiles_wide, CLIPS, HEADS, FRAMES * TILE_S * TILE_S, HD)

def reference(latents, input_weight, norm_gains, output_weight):
    tiles_high = HEIGHT // TILE_S
    tiles_wide = WIDTH // TILE_S
    tile_len = FRAMES * TILE_S * TILE_S
    projected = jnp.dot(latents.reshape(-1, D), input_weight.reshape(D, 3 * HEADS * HD), preferred_element_type=jnp.float32)
    projected = projected.reshape(CLIPS, FRAMES, HEIGHT, WIDTH, 3, HEADS, HD)
    queries = rms_norm(projected[:, :, :, :, 0], norm_gains[0]).astype(jnp.bfloat16)
    keys_all = rms_norm(projected[:, :, :, :, 1], norm_gains[1]).astype(jnp.bfloat16)
    values_all = projected[:, :, :, :, 2].astype(jnp.bfloat16)
    query_tiles = to_tiles(queries, tiles_high, tiles_wide)
    padding = ((1, 1), (1, 1), (0, 0), (0, 0), (0, 0), (0, 0))
    key_tiles = jnp.pad(to_tiles(keys_all, tiles_high, tiles_wide), padding)
    value_tiles = jnp.pad(to_tiles(values_all, tiles_high, tiles_wide), padding)
    present = jnp.pad(jnp.ones((tiles_high, tiles_wide), jnp.int32), 1)
    frame_tile = jnp.repeat(jnp.arange(FRAMES, dtype=jnp.int32) // TILE_T, TILE_S * TILE_S)
    near_time = jnp.abs(frame_tile[:, None] - frame_tile[None, :]) <= 1
    inv_root = 1.0 / math.sqrt(HD)

    def one_tile(index):
        zero_at = jnp.zeros((), jnp.int32)
        row_at = (index // tiles_wide).astype(jnp.int32)
        col_at = (index % tiles_wide).astype(jnp.int32)
        own_query = lax.dynamic_slice(query_tiles, (row_at, col_at, zero_at, zero_at, zero_at, zero_at), (1, 1, CLIPS, HEADS, tile_len, HD))
        own_query = own_query.reshape(CLIPS, HEADS, tile_len, HD)
        near_keys = lax.dynamic_slice(key_tiles, (row_at, col_at, zero_at, zero_at, zero_at, zero_at), (3, 3, CLIPS, HEADS, tile_len, HD))
        near_keys = near_keys.transpose(2, 3, 0, 1, 4, 5).reshape(CLIPS, HEADS, 9 * tile_len, HD)
        near_values = lax.dynamic_slice(value_tiles, (row_at, col_at, zero_at, zero_at, zero_at, zero_at), (3, 3, CLIPS, HEADS, tile_len, HD))
        near_values = near_values.transpose(2, 3, 0, 1, 4, 5).reshape(CLIPS, HEADS, 9 * tile_len, HD)
        exists = lax.dynamic_slice(present, (row_at, col_at), (3, 3)).reshape(9)
        allowed = jnp.tile(near_time, (1, 9)) & (jnp.repeat(exists, tile_len) > 0)[None, :]
        scores = jnp.einsum('chqd,chkd->chqk', own_query.astype(jnp.float32), near_keys.astype(jnp.float32)) * inv_root
        scores = jnp.where(allowed[None, None], scores, -1e+30)
        row_peak = lax.optimization_barrier(jnp.max(scores, axis=-1, keepdims=True))
        weights = jnp.exp(scores - row_peak)
        probability = (weights / lax.optimization_barrier(jnp.sum(weights, axis=-1, keepdims=True))).astype(jnp.bfloat16)
        attended = jnp.einsum('chqk,chkd->chqd', probability.astype(jnp.float32), near_values.astype(jnp.float32))
        return attended.astype(jnp.bfloat16)
    attended = lax.map(one_tile, jnp.arange(tiles_high * tiles_wide, dtype=jnp.int32))
    attended = attended.reshape(tiles_high, tiles_wide, CLIPS, HEADS, FRAMES, TILE_S, TILE_S, HD)
    attended = attended.transpose(2, 4, 0, 5, 1, 6, 3, 7).reshape(-1, HEADS * HD)
    mixed = jnp.dot(attended, output_weight.reshape(HEADS * HD, D), preferred_element_type=jnp.float32)
    return mixed.astype(jnp.bfloat16).reshape(CLIPS, FRAMES, HEIGHT, WIDTH, D)
```

```python
import functools
import math

import jax
import jax.numpy as jnp
from jax import lax
from jax.experimental import pallas as pl
from jax.experimental.pallas import tpu as pltpu
from jax.sharding import PartitionSpec as P

TILE_T = 4


EPSILON = 1e-06


def padded(cells, sides, width):
    for axis, dim in sides:
        count = lax.axis_size(axis)
        ends = count - 1
        head = lax.slice_in_dim(cells, 0, width, axis=dim)
        tail = lax.slice_in_dim(cells, cells.shape[dim] - width, cells.shape[dim], axis=dim)
        cells = jnp.concatenate(
            [
                lax.ppermute(tail, axis, [(i, (i + 1) % count) for i in range(ends)]),
                cells,
                lax.ppermute(head, axis, [((i + 1) % count, i) for i in range(ends)]),
            ],
            axis=dim,
        )
    return cells


def rms_norm(values, gain_row):
    mean_square = jnp.mean(values * values, axis=-1, keepdims=True)
    return values * lax.rsqrt(mean_square + EPSILON) * gain_row


def halo_plan(latents, input_weight, norm_gains, output_weight):
    clip_count = latents.shape[0]
    frames_local = latents.shape[1]
    tile_side = latents.shape[2]
    model_width = latents.shape[4]
    heads_local = input_weight.shape[2]
    head_dim = input_weight.shape[3]
    projected = jnp.einsum(
        "cfhwd,dsne->cfhwsne",
        lax.all_gather(latents, "ta", axis=1, tiled=True),
        input_weight,
        preferred_element_type=jnp.float32,
    )
    query_normed = rms_norm(projected[:, :, :, :, 0], norm_gains[0])
    key_normed = rms_norm(projected[:, :, :, :, 1], norm_gains[1])
    stacked = jnp.stack([query_normed, key_normed, projected[:, :, :, :, 2]], axis=4).astype(
        jnp.bfloat16
    )
    frames = stacked.shape[1]
    query_all = stacked[:, :, :, :, 0]
    key_value = stacked[:, :, :, :, 1:]
    beside_all = padded(key_value, (("ha", 2), ("wa", 3)), tile_side)
    height_index = lax.axis_index("ha")
    width_index = lax.axis_index("wa")
    band_rows = jnp.stack(
        [height_index > 0, height_index >= 0, height_index < lax.axis_size("ha") - 1]
    )
    band_cols = jnp.stack(
        [width_index > 0, width_index >= 0, width_index < lax.axis_size("wa") - 1]
    )
    rows_valid = jnp.repeat(band_rows, tile_side)
    cols_valid = jnp.repeat(band_cols, tile_side)
    around_mask = (rows_valid[:, None] & cols_valid[None, :]).reshape(-1)
    spatial = tile_side * tile_side
    around_len = 9 * spatial
    queries = query_all.reshape(clip_count, frames, spatial, heads_local, head_dim)
    keys_all = beside_all[:, :, :, :, 0].reshape(
        clip_count, frames, around_len, heads_local, head_dim
    )
    values_all = beside_all[:, :, :, :, 1].reshape(
        clip_count, frames, around_len, heads_local, head_dim
    )
    inv_root = 1.0 / math.sqrt(head_dim)
    tile_count = -(-frames // TILE_T)
    pieces = []
    for tile_at in range(tile_count):
        query_low = tile_at * TILE_T
        query_high = min(query_low + TILE_T, frames)
        key_low = max(query_low - TILE_T, 0)
        key_high = min(query_low + 2 * TILE_T, frames)
        query_block = queries[:, query_low:query_high].reshape(
            clip_count, (query_high - query_low) * spatial, heads_local, head_dim
        )
        key_block = keys_all.reshape(
            clip_count, (key_high - key_low) * around_len, heads_local, head_dim
        )
        value_block = values_all.reshape(
            clip_count, (key_high - key_low) * around_len, heads_local, head_dim
        )
        key_mask = jnp.tile(around_mask, key_high - key_low)
        scores = (
            jnp.einsum(
                "cqnd,cknd->ncqk", query_block, key_block, preferred_element_type=jnp.float32
            )
            * inv_root
        )
        scores = jnp.where(key_mask, scores, -1e30)
        row_peak = jnp.max(scores, axis=-1, keepdims=True)
        weights = jnp.exp(scores - row_peak)
        probability = (weights / jnp.sum(weights, axis=-1, keepdims=True)).astype(jnp.bfloat16)
        pieces.append(
            jnp.einsum(
                "ncqk,cknd->ncqd", probability, value_block, preferred_element_type=jnp.float32
            ).astype(jnp.bfloat16)
        )
    attended = jnp.concatenate(pieces, axis=2).reshape(
        heads_local, clip_count, frames, spatial, head_dim
    )
    own_rows = lax.psum_scatter(
        jnp.einsum("ncfqd,nde->fcqe", attended, output_weight, preferred_element_type=jnp.float32),
        "ta",
        scatter_dimension=0,
        tiled=True,
    )
    result = own_rows.transpose(1, 0, 2, 3).reshape(
        clip_count, frames_local, tile_side, tile_side, model_width
    )
    return result.astype(jnp.bfloat16)


def shift_perm(count, by):
    return [(i, (i + by) % count) for i in range(count)]


def attention_kernel(groups, columns, scale, valid_ref, query_ref, *refs):
    kv_refs, out_ref, peak_ref, total_ref, sum_ref = refs[:-4], refs[-4], refs[-3], refs[-2], refs[-1]
    column = pl.program_id(1)
    edge = (column == 0) | (column == columns - 1)
    to_exp2 = scale * math.log2(math.e)

    def one_row(row, start, width):
        query = query_ref[0, 0, 0]
        scores, values = [], []
        for group in range(groups):
            ref = kv_refs[row * groups + group]
            tokens = ref.shape[3]
            first = ref.shape[2] - 2
            key = ref[pl.ds(start, width), 0, first].reshape(width * tokens, -1)
            values.append(ref[pl.ds(start, width), 0, first + 1].reshape(width * tokens, -1))
            scores.append(
                lax.dot_general(
                    query, key, (((1,), (1,)), ((), ())), preferred_element_type=jnp.float32
                )
            )
        peak = scores[0].max(axis=1, keepdims=True)
        for score in scores[1:]:
            peak = jnp.maximum(peak, score.max(axis=1, keepdims=True))
        if row > 0:
            before = peak_ref[...]
            peak = jnp.maximum(peak, before)
            fade = jnp.exp2((before - peak) * to_exp2)
        offset = peak * to_exp2
        total, summed = 0.0, 0.0
        for score, value in zip(scores, values):
            weight = jnp.exp2(score * to_exp2 - offset)
            total = total + weight.sum(axis=1, keepdims=True)
            summed = summed + jnp.dot(
                weight.astype(jnp.bfloat16), value, preferred_element_type=jnp.float32
            )
        if row > 0:
            total = total + total_ref[...] * fade
            summed = summed + sum_ref[...] * fade
        peak_ref[...] = peak
        total_ref[...] = total
        sum_ref[...] = summed

    def all_rows(start, width):
        one_row(0, start, width)
        for row in (1, 2):
            pl.when(valid_ref[row - 1] > 0)(lambda row=row: one_row(row, start, width))

    pl.when(edge)(lambda: all_rows(jnp.where(column == 0, 0, columns - 2), 2))
    pl.when(jnp.logical_not(edge))(lambda: all_rows(column - 1, 3))
    out_ref[0, 0] = (sum_ref[...] / total_ref[...]).astype(out_ref.dtype)


def attend(valid, stream, rows, scale):
    columns, heads, _, tokens, head_dim = stream.shape
    groups = len(rows) // 3
    keys = sum(kv.shape[3] for kv in rows) * 10 // 4

    def kv_spec(kv):
        return pl.BlockSpec(
            (columns, 1, kv.shape[2], kv.shape[3], head_dim), lambda h, c, v: (0, h, 0, 0, 0)
        )

    pairs = heads * columns * tokens * keys
    return pl.pallas_call(
        functools.partial(attention_kernel, groups, columns, scale),
        grid_spec=pltpu.PrefetchScalarGridSpec(
            num_scalar_prefetch=1,
            grid=(heads, columns),
            in_specs=[
                pl.BlockSpec((1, 1, 1, tokens, head_dim), lambda h, c, v: (c, h, 0, 0, 0))
            ]
            + [kv_spec(kv) for kv in rows],
            out_specs=pl.BlockSpec((1, 1, tokens, head_dim), lambda h, c, v: (c, h, 0, 0)),
            scratch_shapes=[
                pltpu.VMEM((tokens, 1), jnp.float32),
                pltpu.VMEM((tokens, 1), jnp.float32),
                pltpu.VMEM((tokens, head_dim), jnp.float32),
            ],
        ),
        out_shape=jax.ShapeDtypeStruct((columns, heads, tokens, head_dim), jnp.bfloat16),
        cost_estimate=pl.CostEstimate(
            flops=pairs * head_dim * 8, bytes_accessed=pairs * 4, transcendentals=pairs
        ),
        name="tile_attention",
    )(valid, stream, *rows)


def row_plan(latents, input_weight, norm_gains, output_weight):
    frame_parts = lax.axis_size("ta")
    row_parts = lax.axis_size("ha")
    col_parts = lax.axis_size("wa")
    model_width = latents.shape[-1]
    tokens = math.prod(latents.shape[:-1])
    heads_local, head_dim = input_weight.shape[2:]
    heads_each = heads_local // col_parts
    own = latents.reshape(tokens, model_width)
    groups = [own]
    for by in range(1, frame_parts):
        groups.append(lax.ppermute(own, "ta", shift_perm(frame_parts, by)))
    gains = jnp.concatenate([norm_gains, jnp.ones_like(norm_gains[:1])])[:, None, :]
    is_value = jnp.arange(3).reshape(3, 1, 1) == 2

    def project(group):
        projected = jnp.einsum(
            "td,dsne->nste", group, input_weight, preferred_element_type=jnp.float32
        )
        mean_square = jnp.mean(projected * projected, axis=-1, keepdims=True)
        factor = jnp.where(is_value, 1.0, lax.rsqrt(mean_square + EPSILON))
        normed = (projected * factor * gains).astype(jnp.bfloat16)
        dealt = normed.reshape(col_parts, heads_each, 3, tokens, head_dim)
        return lax.all_to_all(dealt, "wa", 0, 0)

    streams = [project(group) for group in groups]
    down = [(i, i + 1) for i in range(row_parts - 1)]
    up = [(i + 1, i) for i in range(row_parts - 1)]
    rows = list(streams)
    for perm in (down, up):
        rows += [lax.ppermute(stream[:, :, 1:], "ha", perm) for stream in streams]
    height_index = lax.axis_index("ha")
    valid = jnp.stack([height_index > 0, height_index < row_parts - 1]).astype(jnp.int32)
    scale = 1.0 / math.sqrt(head_dim)

    def shares(stream):
        attended = lax.all_to_all(attend(valid, stream, rows, scale), "wa", 0, 0)
        attended = attended.reshape(heads_local, tokens, head_dim)
        return jnp.einsum(
            "nte,ned->td", attended, output_weight, preferred_element_type=jnp.float32
        )

    arrived = []
    for by in range(1, frame_parts):
        share = shares(streams[by]).astype(jnp.bfloat16)
        arrived.append(lax.ppermute(share, "ta", shift_perm(frame_parts, -by)))
    result = shares(streams[0])
    for share in arrived:
        result = result + share.astype(jnp.float32)
    return result.astype(jnp.bfloat16).reshape(latents.shape)


def solution(mesh):
    in_specs = (
        P(None, "ta", "ha", "wa", None),
        P(None, None, "ta", None),
        P(),
        P("ta", None, None),
    )
    out_specs = P(None, "ta", "ha", "wa", None)

    def per_device(latents, input_weight, norm_gains, output_weight):
        frames = latents.shape[1] * lax.axis_size("ta")
        dealt_heads = input_weight.shape[2] % lax.axis_size("wa") == 0
        if latents.shape[0] == 1 and dealt_heads and frames <= 2 * TILE_T:
            return row_plan(latents, input_weight, norm_gains, output_weight)
        return halo_plan(latents, input_weight, norm_gains, output_weight)

    return jax.shard_map(
        per_device, mesh=mesh, in_specs=in_specs, out_specs=out_specs, check_vma=False
    )
```

```python
import functools
import math

import jax
import jax.numpy as jnp
from jax import lax
from jax.experimental import pallas as pl
from jax.experimental.pallas import tpu as pltpu
from jax.sharding import PartitionSpec as P


TILE_T = 4


EPSILON = 1e-06


def padded(cells, sides, width):
    for axis, dim in sides:
        count = lax.axis_size(axis)
        ends = count - 1
        head = lax.slice_in_dim(cells, 0, width, axis=dim)
        tail = lax.slice_in_dim(cells, cells.shape[dim] - width, cells.shape[dim], axis=dim)
        cells = jnp.concatenate(
            [
                lax.ppermute(tail, axis, [(i, (i + 1) % count) for i in range(ends)]),
                cells,
                lax.ppermute(head, axis, [((i + 1) % count, i) for i in range(ends)]),
            ],
            axis=dim,
        )
    return cells


def rms_norm(values, gain_row):
    mean_square = jnp.mean(values * values, axis=-1, keepdims=True)
    return values * lax.rsqrt(mean_square + EPSILON) * gain_row


def halo_plan(latents, input_weight, norm_gains, output_weight):
    clip_count = latents.shape[0]
    frames_local = latents.shape[1]
    tile_side = latents.shape[2]
    model_width = latents.shape[4]
    heads_local = input_weight.shape[2]
    head_dim = input_weight.shape[3]
    projected = jnp.einsum(
        "cfhwd,dsne->cfhwsne",
        lax.all_gather(latents, "ta", axis=1, tiled=True),
        input_weight,
        preferred_element_type=jnp.float32,
    )
    query_normed = rms_norm(projected[:, :, :, :, 0], norm_gains[0])
    key_normed = rms_norm(projected[:, :, :, :, 1], norm_gains[1])
    stacked = jnp.stack([query_normed, key_normed, projected[:, :, :, :, 2]], axis=4).astype(
        jnp.bfloat16
    )
    frames = stacked.shape[1]
    query_all = stacked[:, :, :, :, 0]
    key_value = stacked[:, :, :, :, 1:]
    beside_all = padded(key_value, (("ha", 2), ("wa", 3)), tile_side)
    height_index = lax.axis_index("ha")
    width_index = lax.axis_index("wa")
    band_rows = jnp.stack(
        [height_index > 0, height_index >= 0, height_index < lax.axis_size("ha") - 1]
    )
    band_cols = jnp.stack(
        [width_index > 0, width_index >= 0, width_index < lax.axis_size("wa") - 1]
    )
    rows_valid = jnp.repeat(band_rows, tile_side)
    cols_valid = jnp.repeat(band_cols, tile_side)
    around_mask = (rows_valid[:, None] & cols_valid[None, :]).reshape(-1)
    spatial = tile_side * tile_side
    around_len = 9 * spatial
    queries = query_all.reshape(clip_count, frames, spatial, heads_local, head_dim)
    keys_all = beside_all[:, :, :, :, 0].reshape(
        clip_count, frames, around_len, heads_local, head_dim
    )
    values_all = beside_all[:, :, :, :, 1].reshape(
        clip_count, frames, around_len, heads_local, head_dim
    )
    inv_root = 1.0 / math.sqrt(head_dim)
    tile_count = -(-frames // TILE_T)
    pieces = []
    for tile_at in range(tile_count):
        query_low = tile_at * TILE_T
        query_high = min(query_low + TILE_T, frames)
        key_low = max(query_low - TILE_T, 0)
        key_high = min(query_low + 2 * TILE_T, frames)
        query_block = queries[:, query_low:query_high].reshape(
            clip_count, (query_high - query_low) * spatial, heads_local, head_dim
        )
        key_block = keys_all.reshape(
            clip_count, (key_high - key_low) * around_len, heads_local, head_dim
        )
        value_block = values_all.reshape(
            clip_count, (key_high - key_low) * around_len, heads_local, head_dim
        )
        key_mask = jnp.tile(around_mask, key_high - key_low)
        scores = (
            jnp.einsum(
                "cqnd,cknd->ncqk", query_block, key_block, preferred_element_type=jnp.float32
            )
            * inv_root
        )
        scores = jnp.where(key_mask, scores, -1e30)
        row_peak = jnp.max(scores, axis=-1, keepdims=True)
        weights = jnp.exp(scores - row_peak)
        probability = (weights / jnp.sum(weights, axis=-1, keepdims=True)).astype(jnp.bfloat16)
        pieces.append(
            jnp.einsum(
                "ncqk,cknd->ncqd", probability, value_block, preferred_element_type=jnp.float32
            ).astype(jnp.bfloat16)
        )
    attended = jnp.concatenate(pieces, axis=2).reshape(
        heads_local, clip_count, frames, spatial, head_dim
    )
    own_rows = lax.psum_scatter(
        jnp.einsum("ncfqd,nde->fcqe", attended, output_weight, preferred_element_type=jnp.float32),
        "ta",
        scatter_dimension=0,
        tiled=True,
    )
    result = own_rows.transpose(1, 0, 2, 3).reshape(
        clip_count, frames_local, tile_side, tile_side, model_width
    )
    return result.astype(jnp.bfloat16)


def shift_perm(count, by):
    return [(i, (i + by) % count) for i in range(count)]


def after(value, earlier):
    return lax.optimization_barrier((value, earlier))[0]


def attention_kernel(parts, columns, scale, first, last, valid_ref, *refs):
    queries = refs[: parts]
    rest = refs[parts:]
    if not first:
        before_ref, rest = rest[0], rest[1:]
    kv_refs, out_ref, state_ref = rest[:-2], rest[-2], rest[-1]
    groups = len(kv_refs) // 3
    head_dim = queries[0].shape[-1]
    column = pl.program_id(1)
    edge = (column == 0) | (column == columns - 1)
    to_exp2 = scale * math.log2(math.e)
    state_ref = state_ref if last else out_ref.at[0, 0]

    def one_row(row, start, width):
        query = jnp.concatenate([ref[0, 0, 0] for ref in queries], axis=0)
        scores, values = [], []
        for group in range(groups):
            ref = kv_refs[row * groups + group]
            tokens = ref.shape[3]
            at = ref.shape[2] - 2
            key = ref[pl.ds(start, width), 0, at].reshape(width * tokens, head_dim)
            values.append(ref[pl.ds(start, width), 0, at + 1].reshape(width * tokens, head_dim))
            scores.append(
                lax.dot_general(
                    query, key, (((1,), (1,)), ((), ())), preferred_element_type=jnp.float32
                )
            )
        peak = scores[0].max(axis=1, keepdims=True)
        for score in scores[1:]:
            peak = jnp.maximum(peak, score.max(axis=1, keepdims=True))
        fresh = first and row == 0
        old_ref = state_ref if row > 0 or first else before_ref.at[0, 0]
        if not fresh:
            old_peak = old_ref[:, head_dim : head_dim + 1]
            peak = jnp.maximum(peak, old_peak)
            fade = jnp.exp2((old_peak - peak) * to_exp2)
        offset = peak * to_exp2
        total, summed = 0.0, 0.0
        for score, value in zip(scores, values):
            weight = jnp.exp2(score * to_exp2 - offset)
            total = total + weight.sum(axis=1, keepdims=True)
            summed = summed + jnp.dot(
                weight.astype(jnp.bfloat16), value, preferred_element_type=jnp.float32
            )
        if not fresh:
            total = total + old_ref[:, head_dim + 1 : head_dim + 2] * fade
            summed = summed + old_ref[:, :head_dim] * fade
        state_ref[:, :head_dim] = summed
        state_ref[:, head_dim : head_dim + 1] = peak
        state_ref[:, head_dim + 1 : head_dim + 2] = total

    def all_rows(start, width):
        one_row(0, start, width)
        for row in (1, 2):
            pl.when(valid_ref[row - 1] > 0)(lambda row=row: one_row(row, start, width))

    pl.when(edge)(lambda: all_rows(jnp.where(column == 0, 0, columns - 2), 2))
    pl.when(jnp.logical_not(edge))(lambda: all_rows(column - 1, 3))
    if last:
        out = state_ref[:, :head_dim] / state_ref[:, head_dim + 1 : head_dim + 2]
        places, each = out_ref.shape[0], out_ref.shape[3]
        for by in range(places):
            out_ref[valid_ref[2 + by], 0, 0] = out[by * each : (by + 1) * each].astype(out_ref.dtype)


def attend(valid, streams, before, rows, scale, last, places):
    columns, heads, _, _, head_dim = streams[0].shape
    tokens = sum(stream.shape[3] for stream in streams)
    keys = sum(kv.shape[3] for kv in rows) * 10 // 4
    first = before is None

    def at_query(h, c, v):
        return (c, h, 0, 0)

    def kv_spec(kv):
        return pl.BlockSpec(
            (columns, 1, kv.shape[2], kv.shape[3], head_dim), lambda h, c, v: (0, h, 0, 0, 0)
        )

    if last:
        each = tokens // places
        out_spec = pl.BlockSpec((places, 1, 1, each, head_dim), lambda h, c, v: (0, c, h, 0, 0))
        out_shape = jax.ShapeDtypeStruct((places, columns, heads, each, head_dim), jnp.bfloat16)
    else:
        out_spec = pl.BlockSpec((1, 1, tokens, 2 * head_dim), at_query)
        out_shape = jax.ShapeDtypeStruct((columns, heads, tokens, 2 * head_dim), jnp.float32)
    pairs = heads * columns * tokens * keys
    state = [] if first else [before]
    return pl.pallas_call(
        functools.partial(attention_kernel, len(streams), columns, scale, first, last),
        grid_spec=pltpu.PrefetchScalarGridSpec(
            num_scalar_prefetch=1,
            grid=(heads, columns),
            in_specs=[
                pl.BlockSpec((1, 1, 1, stream.shape[3], head_dim), lambda h, c, v: (c, h, 0, 0, 0))
                for stream in streams
            ]
            + [pl.BlockSpec((1, 1, tokens, 2 * head_dim), at_query) for _ in state]
            + [kv_spec(kv) for kv in rows],
            out_specs=out_spec,
            scratch_shapes=[pltpu.VMEM((tokens, 2 * head_dim), jnp.float32)],
        ),
        out_shape=out_shape,
        cost_estimate=pl.CostEstimate(
            flops=pairs * head_dim * 8, bytes_accessed=pairs * 4, transcendentals=pairs
        ),
        name="tile_attention",
    )(valid, *streams, *state, *rows)


def mix_kernel(at_ref, attended_ref, *refs):
    weight_refs, out_ref = refs[:-1], refs[-1]
    places = []
    for ref in weight_refs:
        for k in range(ref.shape[0]):
            places.append((ref, k))
    total = 0.0
    for at in range(0, len(places), 2):
        pair = places[at : at + 2]
        left = jnp.concatenate([attended_ref[at_ref[at + i]] for i in range(len(pair))], axis=1)
        right = jnp.concatenate([ref[k] for ref, k in pair], axis=0)
        total = total + jnp.dot(left, right, preferred_element_type=jnp.float32)
    out_ref[...] = total.astype(out_ref.dtype)


def mix(order, attended, weights):
    heads, tokens, head_dim = attended.shape
    width = weights[0].shape[-1]
    step = math.gcd(width, 768)
    return pl.pallas_call(
        mix_kernel,
        grid_spec=pltpu.PrefetchScalarGridSpec(
            num_scalar_prefetch=1,
            grid=(width // step,),
            in_specs=[pl.BlockSpec(attended.shape, lambda i, o: (0, 0, 0))]
            + [
                pl.BlockSpec((weight.shape[0], head_dim, step), lambda i, o: (0, 0, i))
                for weight in weights
            ],
            out_specs=pl.BlockSpec((tokens, step), lambda i, o: (0, i)),
        ),
        out_shape=jax.ShapeDtypeStruct((tokens, width), jnp.bfloat16),
        cost_estimate=pl.CostEstimate(
            flops=2 * heads * tokens * head_dim * width,
            bytes_accessed=2 * heads * head_dim * width,
            transcendentals=0,
        ),
        name="mix_heads",
    )(order, attended, *weights)


def row_plan(latents, input_weight, norm_gains, output_weight):
    frame_parts = lax.axis_size("ta")
    row_parts = lax.axis_size("ha")
    col_parts = lax.axis_size("wa")
    frames = latents.shape[1]
    heads_local, head_dim = input_weight.shape[2:]
    heads_each = heads_local // col_parts
    here, column_at = lax.axis_index("ta"), lax.axis_index("wa")
    cuts = 2 if frames % 2 == 0 else 1
    step = frames // cuts
    own = [lax.slice_in_dim(latents, i * step, (i + 1) * step, axis=1) for i in range(cuts)]
    chunks = [latents]
    for by in range(1, frame_parts):
        for chunk in own:
            chunks.append(lax.ppermute(chunk, "ta", shift_perm(frame_parts, by)))

    fetched = []
    for by in range(1, frame_parts):
        for k in range(heads_each):
            share = lax.dynamic_slice_in_dim(output_weight, column_at * heads_each + k, 1, axis=0)
            share = lax.ppermute(after(share, chunks[-1]), "ta", shift_perm(frame_parts, by))
            fetched.append((by, k, share))

    def project(chunk):
        projected = jnp.einsum(
            "cfhwd,dsne->cfhwsne", chunk, input_weight, preferred_element_type=jnp.float32
        )
        normed = jnp.stack(
            [
                rms_norm(projected[:, :, :, :, 0], norm_gains[0]),
                rms_norm(projected[:, :, :, :, 1], norm_gains[1]),
                projected[:, :, :, :, 2],
            ]
        ).astype(jnp.bfloat16)
        return normed.transpose(5, 0, 1, 2, 3, 4, 6)

    streams = []
    ready = None
    for at, chunk in enumerate(chunks):
        if ready is not None:
            chunk = after(chunk, ready)
        ready = project(chunk)
        for part in range(cuts if at == 0 else 1):
            dealt = lax.slice_in_dim(ready, part * step, (part + 1) * step, axis=3)
            dealt = dealt.reshape(col_parts, heads_each, 3, -1, head_dim)
            streams.append(lax.all_to_all(dealt, "wa", 0, 0))
    down = [(i, i + 1) for i in range(row_parts - 1)]
    up = [(i + 1, i) for i in range(row_parts - 1)]
    above, below = [], []
    for stream in streams:
        above.append(lax.ppermute(stream[:, :, 1:], "ha", down))
        below.append(lax.ppermute(stream[:, :, 1:], "ha", up))
    height_index = lax.axis_index("ha")
    places = [lax.rem(here + (frame_parts - by), frame_parts) for by in range(frame_parts)]
    scalars = jnp.stack(
        [(height_index > 0).astype(jnp.int32), (height_index < row_parts - 1).astype(jnp.int32)]
        + places
    )
    scale = 1.0 / math.sqrt(head_dim)

    def spread(block):
        held = [(0, block)]
        distance = col_parts // 2
        while distance:
            perm = [(i, i ^ distance) for i in range(col_parts)]
            got = lax.ppermute(jnp.concatenate([b for _, b in held], axis=0), "wa", perm)
            held = held + [
                (mask ^ distance, got[i : i + 1]) for i, (mask, _) in enumerate(held)
            ]
            distance //= 2
        return held

    state = attend(
        scalars, streams, None, streams[:cuts] + above[:cuts] + below[:cuts], scale, False, 1
    )
    attended = attend(
        scalars, streams, state, streams[cuts:] + above[cuts:] + below[cuts:], scale, True,
        frame_parts,
    )
    sent = attended.reshape(frame_parts * col_parts, heads_each, -1, head_dim)
    got = lax.all_to_all(sent, ("ta", "wa"), 0, 0)
    got = got.reshape(frame_parts * heads_local, -1, head_dim)
    order = [here * heads_local + k for k in range(heads_local)]
    weights = [output_weight]
    for by, k, block in fetched:
        for mask, part in spread(block):
            weights.append(part)
            order.append(
                places[by] * heads_local + (column_at ^ mask) * heads_each + k
            )
    result = mix(jnp.stack(order).astype(jnp.int32), got, weights)
    return result.reshape(latents.shape)


def solution(mesh):
    in_specs = (
        P(None, "ta", "ha", "wa", None),
        P(None, None, "ta", None),
        P(),
        P("ta", None, None),
    )
    out_specs = P(None, "ta", "ha", "wa", None)

    def per_device(latents, input_weight, norm_gains, output_weight):
        frames = latents.shape[1] * lax.axis_size("ta")
        width = lax.axis_size("wa")
        dealt_heads = input_weight.shape[2] % width == 0 and width & (width - 1) == 0
        if latents.shape[0] == 1 and dealt_heads and frames <= 2 * TILE_T:
            return row_plan(latents, input_weight, norm_gains, output_weight)
        return halo_plan(latents, input_weight, norm_gains, output_weight)

    return jax.shard_map(
        per_device, mesh=mesh, in_specs=in_specs, out_specs=out_specs, check_vma=False
    )
```

```python
import functools
import math

import jax
import jax.numpy as jnp
from jax import lax
from jax.experimental import pallas as pl
from jax.experimental.pallas import tpu as pltpu
from jax.sharding import PartitionSpec as P


TILE_T = 4


EPSILON = 1e-06


def padded(cells, sides, width):
    for axis, dim in sides:
        count = lax.axis_size(axis)
        ends = count - 1
        head = lax.slice_in_dim(cells, 0, width, axis=dim)
        tail = lax.slice_in_dim(cells, cells.shape[dim] - width, cells.shape[dim], axis=dim)
        cells = jnp.concatenate(
            [
                lax.ppermute(tail, axis, [(i, (i + 1) % count) for i in range(ends)]),
                cells,
                lax.ppermute(head, axis, [((i + 1) % count, i) for i in range(ends)]),
            ],
            axis=dim,
        )
    return cells


def rms_norm(values, gain_row):
    mean_square = jnp.mean(values * values, axis=-1, keepdims=True)
    return values * lax.rsqrt(mean_square + EPSILON) * gain_row


def halo_plan(latents, input_weight, norm_gains, output_weight):
    clip_count = latents.shape[0]
    frames_local = latents.shape[1]
    tile_side = latents.shape[2]
    model_width = latents.shape[4]
    heads_local = input_weight.shape[2]
    head_dim = input_weight.shape[3]
    projected = jnp.einsum(
        "cfhwd,dsne->cfhwsne",
        lax.all_gather(latents, "ta", axis=1, tiled=True),
        input_weight,
        preferred_element_type=jnp.float32,
    )
    query_normed = rms_norm(projected[:, :, :, :, 0], norm_gains[0])
    key_normed = rms_norm(projected[:, :, :, :, 1], norm_gains[1])
    stacked = jnp.stack([query_normed, key_normed, projected[:, :, :, :, 2]], axis=4).astype(
        jnp.bfloat16
    )
    frames = stacked.shape[1]
    query_all = stacked[:, :, :, :, 0]
    key_value = stacked[:, :, :, :, 1:]
    beside_all = padded(key_value, (("ha", 2), ("wa", 3)), tile_side)
    height_index = lax.axis_index("ha")
    width_index = lax.axis_index("wa")
    band_rows = jnp.stack(
        [height_index > 0, height_index >= 0, height_index < lax.axis_size("ha") - 1]
    )
    band_cols = jnp.stack(
        [width_index > 0, width_index >= 0, width_index < lax.axis_size("wa") - 1]
    )
    rows_valid = jnp.repeat(band_rows, tile_side)
    cols_valid = jnp.repeat(band_cols, tile_side)
    around_mask = (rows_valid[:, None] & cols_valid[None, :]).reshape(-1)
    spatial = tile_side * tile_side
    around_len = 9 * spatial
    queries = query_all.reshape(clip_count, frames, spatial, heads_local, head_dim)
    keys_all = beside_all[:, :, :, :, 0].reshape(
        clip_count, frames, around_len, heads_local, head_dim
    )
    values_all = beside_all[:, :, :, :, 1].reshape(
        clip_count, frames, around_len, heads_local, head_dim
    )
    inv_root = 1.0 / math.sqrt(head_dim)
    tile_count = -(-frames // TILE_T)
    pieces = []
    for tile_at in range(tile_count):
        query_low = tile_at * TILE_T
        query_high = min(query_low + TILE_T, frames)
        key_low = max(query_low - TILE_T, 0)
        key_high = min(query_low + 2 * TILE_T, frames)
        query_block = queries[:, query_low:query_high].reshape(
            clip_count, (query_high - query_low) * spatial, heads_local, head_dim
        )
        key_block = keys_all.reshape(
            clip_count, (key_high - key_low) * around_len, heads_local, head_dim
        )
        value_block = values_all.reshape(
            clip_count, (key_high - key_low) * around_len, heads_local, head_dim
        )
        key_mask = jnp.tile(around_mask, key_high - key_low)
        scores = (
            jnp.einsum(
                "cqnd,cknd->ncqk", query_block, key_block, preferred_element_type=jnp.float32
            )
            * inv_root
        )
        scores = jnp.where(key_mask, scores, -1e30)
        row_peak = jnp.max(scores, axis=-1, keepdims=True)
        weights = jnp.exp(scores - row_peak)
        probability = (weights / jnp.sum(weights, axis=-1, keepdims=True)).astype(jnp.bfloat16)
        pieces.append(
            jnp.einsum(
                "ncqk,cknd->ncqd", probability, value_block, preferred_element_type=jnp.float32
            ).astype(jnp.bfloat16)
        )
    attended = jnp.concatenate(pieces, axis=2).reshape(
        heads_local, clip_count, frames, spatial, head_dim
    )
    own_rows = lax.psum_scatter(
        jnp.einsum("ncfqd,nde->fcqe", attended, output_weight, preferred_element_type=jnp.float32),
        "ta",
        scatter_dimension=0,
        tiled=True,
    )
    result = own_rows.transpose(1, 0, 2, 3).reshape(
        clip_count, frames_local, tile_side, tile_side, model_width
    )
    return result.astype(jnp.bfloat16)


REMOTE_CUTS = 2


def shift_perm(count, by):
    return [(i, (i + by) % count) for i in range(count)]


def after(value, earlier):
    return lax.optimization_barrier((value, earlier))[0]


def attention_kernel(parts, columns, scale, first, last, scalar_ref, *refs):
    queries = refs[:parts]
    rest = refs[parts:]
    if not first:
        before_ref, rest = rest[0], rest[1:]
    kv_refs, out_ref = rest[:-1], rest[-1]
    groups = len(kv_refs) // 3
    head_dim = queries[0].shape[-1]
    at_peak = 2 * head_dim - 1
    to_exp2 = scale * math.log2(math.e)
    column = pl.program_id(1)
    edge = (column == 0) | (column == columns - 1)
    both = scalar_ref[0] > 0

    def block(start, width, rows):
        query = jnp.concatenate([ref[0, 0, 0] for ref in queries], axis=0)
        keys, values = [], []
        for ref in kv_refs[: rows * groups]:
            tokens = ref.shape[3]
            at = ref.shape[2] - 2
            key = ref[pl.ds(start, width), 0, at].reshape(width * tokens, head_dim)
            value = ref[pl.ds(start, width), 0, at + 1].reshape(width * tokens, head_dim)
            keys.append(key)
            values.append(jnp.concatenate([value, jnp.ones_like(value)], axis=1))
        halves = 2
        each = query.shape[0] // halves

        def score(half, key):
            return lax.dot_general(
                query[half * each : (half + 1) * each],
                key,
                (((1,), (1,)), ((), ())),
                preferred_element_type=jnp.float32,
            )

        scores = [score(0, key) for key in keys]
        for half in range(halves):
            here = slice(half * each, (half + 1) * each)
            peak = None
            for part in scores:
                for low in range(0, part.shape[1], head_dim):
                    piece = part[:, low : low + head_dim]
                    peak = piece if peak is None else jnp.maximum(peak, piece)
            peak = peak.max(axis=1, keepdims=True)
            if not first:
                old_peak = before_ref[0, 0, here, at_peak:]
                peak = jnp.maximum(peak, old_peak)
            offset = peak * to_exp2
            summed = None
            ahead = []
            for key, value, part in zip(keys, values, scores):
                if half + 1 < halves:
                    ahead.append(score(half + 1, key))
                weight = jnp.exp2(part * to_exp2 - offset).astype(jnp.bfloat16)
                term = jnp.dot(weight, value, preferred_element_type=jnp.float32)
                summed = term if summed is None else summed + term
            if not first:
                fade = jnp.exp2(old_peak * to_exp2 - offset)
                summed = summed + before_ref[0, 0, here, :] * fade
            if last:
                out = summed[:, :head_dim] / summed[:, head_dim : head_dim + 1]
                out = out.astype(out_ref.dtype)
                piece = out_ref.shape[3]
                size = min(piece, each)
                for low in range(0, each, size):
                    place, at = divmod(half * each + low, piece)
                    out_ref[scalar_ref[1 + place], 0, 0, at : at + size] = out[low : low + size]
            else:
                out_ref[0, 0, here, :] = summed
                out_ref[0, 0, here, at_peak:] = peak
            scores = ahead

    for at_edge in (True, False):
        for rows in (2, 3):
            start = jnp.where(column == 0, 0, columns - 2) if at_edge else column - 1
            case = (edge == at_edge) & (both == (rows == 3))
            pl.when(case)(functools.partial(block, start, 2 if at_edge else 3, rows))


def attend(valid, streams, before, rows, scale, last, places):
    columns, heads, _, _, head_dim = streams[0].shape
    tokens = sum(stream.shape[3] for stream in streams)
    keys = sum(kv.shape[3] for kv in rows) * 10 // 4
    first = before is None

    def at_query(h, c, v):
        return (c, h, 0, 0)

    def kv_spec(kv):
        return pl.BlockSpec(
            (columns, 1, kv.shape[2], kv.shape[3], head_dim), lambda h, c, v: (0, h, 0, 0, 0)
        )

    if last:
        each = tokens // places
        out_spec = pl.BlockSpec((places, 1, 1, each, head_dim), lambda h, c, v: (0, c, h, 0, 0))
        out_shape = jax.ShapeDtypeStruct((places, columns, heads, each, head_dim), jnp.bfloat16)
    else:
        out_spec = pl.BlockSpec((1, 1, tokens, 2 * head_dim), at_query)
        out_shape = jax.ShapeDtypeStruct((columns, heads, tokens, 2 * head_dim), jnp.float32)
    pairs = heads * columns * tokens * keys
    state = [] if first else [before]
    return pl.pallas_call(
        functools.partial(attention_kernel, len(streams), columns, scale, first, last),
        grid_spec=pltpu.PrefetchScalarGridSpec(
            num_scalar_prefetch=1,
            grid=(heads, columns),
            in_specs=[
                pl.BlockSpec((1, 1, 1, stream.shape[3], head_dim), lambda h, c, v: (c, h, 0, 0, 0))
                for stream in streams
            ]
            + [pl.BlockSpec((1, 1, tokens, 2 * head_dim), at_query) for _ in state]
            + [kv_spec(kv) for kv in rows],
            out_specs=out_spec,
        ),
        out_shape=out_shape,
        cost_estimate=pl.CostEstimate(
            flops=pairs * head_dim * 8, bytes_accessed=pairs * 4, transcendentals=pairs
        ),
        name="tile_attention",
    )(valid, *streams, *state, *rows)


def mix_kernel(at_ref, attended_ref, *refs):
    weight_refs, out_ref = refs[:-1], refs[-1]
    places = []
    for ref in weight_refs:
        for k in range(ref.shape[0]):
            places.append((ref, k))
    total = 0.0
    for at in range(0, len(places), 2):
        pair = places[at : at + 2]
        left = jnp.concatenate([attended_ref[at_ref[at + i]] for i in range(len(pair))], axis=1)
        right = jnp.concatenate([ref[k] for ref, k in pair], axis=0)
        total = total + jnp.dot(left, right, preferred_element_type=jnp.float32)
    out_ref[...] = total.astype(out_ref.dtype)


def mix(order, attended, weights):
    heads, tokens, head_dim = attended.shape
    width = weights[0].shape[-1]
    step = math.gcd(width, 768)
    return pl.pallas_call(
        mix_kernel,
        grid_spec=pltpu.PrefetchScalarGridSpec(
            num_scalar_prefetch=1,
            grid=(width // step,),
            in_specs=[pl.BlockSpec(attended.shape, lambda i, o: (0, 0, 0))]
            + [
                pl.BlockSpec((weight.shape[0], head_dim, step), lambda i, o: (0, 0, i))
                for weight in weights
            ],
            out_specs=pl.BlockSpec((tokens, step), lambda i, o: (0, i)),
        ),
        out_shape=jax.ShapeDtypeStruct((tokens, width), jnp.bfloat16),
        cost_estimate=pl.CostEstimate(
            flops=2 * heads * tokens * head_dim * width,
            bytes_accessed=2 * heads * head_dim * width,
            transcendentals=0,
        ),
        name="mix_heads",
    )(order, attended, *weights)


def row_plan(latents, input_weight, norm_gains, output_weight):
    frame_parts = lax.axis_size("ta")
    row_parts = lax.axis_size("ha")
    col_parts = lax.axis_size("wa")
    frames = latents.shape[1]
    heads_local, head_dim = input_weight.shape[2:]
    heads_each = heads_local // col_parts
    here, column_at = lax.axis_index("ta"), lax.axis_index("wa")
    cuts = REMOTE_CUTS if frames % REMOTE_CUTS == 0 else 1
    step = frames // cuts
    own = [lax.slice_in_dim(latents, i * step, (i + 1) * step, axis=1) for i in range(cuts)]
    chunks = [latents]
    for by in range(1, frame_parts):
        for chunk in own:
            chunks.append(lax.ppermute(chunk, "ta", shift_perm(frame_parts, by)))

    fetched = []
    for by in range(1, frame_parts):
        for k in range(heads_each):
            share = lax.dynamic_slice_in_dim(output_weight, column_at * heads_each + k, 1, axis=0)
            share = lax.ppermute(after(share, chunks[-1]), "ta", shift_perm(frame_parts, by))
            fetched.append((by, k, share))

    def project(chunk):
        projected = jnp.einsum(
            "cfhwd,dsne->cfhwsne", chunk, input_weight, preferred_element_type=jnp.float32
        )
        normed = jnp.stack(
            [
                rms_norm(projected[:, :, :, :, 0], norm_gains[0]),
                rms_norm(projected[:, :, :, :, 1], norm_gains[1]),
                projected[:, :, :, :, 2],
            ]
        ).astype(jnp.bfloat16)
        return normed.transpose(5, 0, 1, 2, 3, 4, 6)

    streams = []
    ready = None
    for chunk in chunks:
        if ready is not None:
            chunk = after(chunk, ready)
        ready = project(chunk)
        dealt = ready.reshape(col_parts, heads_each, 3, -1, head_dim)
        streams.append(lax.all_to_all(dealt, "wa", 0, 0))
    pair = [(i, i ^ 1) for i in range(row_parts)]
    side = [(i, ((i + 1) ^ 1) - 1) for i in range(1, row_parts - 1)]
    side += [(i, i) for i in {0, row_parts - 1}]
    paired, beside = [], []
    for stream in streams:
        keys_values = stream[:, :, 1:]
        paired.append(lax.ppermute(keys_values, "ha", pair))
        beside.append(lax.ppermute(keys_values, "ha", sorted(side)))
    height_index = lax.axis_index("ha")
    inside = (height_index > 0) & (height_index < row_parts - 1)
    places = [lax.rem(here + (frame_parts - by), frame_parts) for by in range(frame_parts)]
    scalars = jnp.stack([inside.astype(jnp.int32)] + places)
    scale = 1.0 / math.sqrt(head_dim)

    def spread(block):
        held = [(0, block)]
        distance = col_parts // 2
        while distance:
            perm = [(i, i ^ distance) for i in range(col_parts)]
            got = []
            for mask, part in held:
                got.append((mask ^ distance, lax.ppermute(part, "wa", perm)))
            held = held + got
            distance //= 2
        return held

    state = attend(scalars, streams, None, [streams[0], paired[0], beside[0]], scale, False, 1)
    attended = attend(
        scalars, streams, state, streams[1:] + paired[1:] + beside[1:], scale, True,
        frame_parts,
    )
    sent = attended.reshape(frame_parts * col_parts, heads_each, -1, head_dim)
    got = lax.all_to_all(sent, ("ta", "wa"), 0, 0)
    got = got.reshape(frame_parts * heads_local, -1, head_dim)
    order = [here * heads_local + k for k in range(heads_local)]
    weights = [output_weight]
    for by, k, block in fetched:
        for mask, part in spread(block):
            weights.append(part)
            order.append(
                places[by] * heads_local + (column_at ^ mask) * heads_each + k
            )
    result = mix(jnp.stack(order).astype(jnp.int32), got, weights)
    return result.reshape(latents.shape)


def solution(mesh):
    in_specs = (
        P(None, "ta", "ha", "wa", None),
        P(None, None, "ta", None),
        P(),
        P("ta", None, None),
    )
    out_specs = P(None, "ta", "ha", "wa", None)

    def per_device(latents, input_weight, norm_gains, output_weight):
        frames = latents.shape[1] * lax.axis_size("ta")
        width = lax.axis_size("wa")
        dealt_heads = input_weight.shape[2] % width == 0 and width & (width - 1) == 0
        dealt_heads &= lax.axis_size("ha") % 2 == 0
        if latents.shape[0] == 1 and dealt_heads and frames <= 2 * TILE_T:
            return row_plan(latents, input_weight, norm_gains, output_weight)
        return halo_plan(latents, input_weight, norm_gains, output_weight)

    return jax.shard_map(
        per_device, mesh=mesh, in_specs=in_specs, out_specs=out_specs, check_vma=False
    )
```

```python
import functools
import math

import jax
import jax.numpy as jnp
from jax import lax
from jax.experimental import pallas as pl
from jax.experimental.pallas import tpu as pltpu
from jax.sharding import PartitionSpec as P


TILE_T = 4


EPSILON = 1e-06


def padded(cells, sides, width):
    for axis, dim in sides:
        count = lax.axis_size(axis)
        ends = count - 1
        head = lax.slice_in_dim(cells, 0, width, axis=dim)
        tail = lax.slice_in_dim(cells, cells.shape[dim] - width, cells.shape[dim], axis=dim)
        cells = jnp.concatenate(
            [
                lax.ppermute(tail, axis, [(i, (i + 1) % count) for i in range(ends)]),
                cells,
                lax.ppermute(head, axis, [((i + 1) % count, i) for i in range(ends)]),
            ],
            axis=dim,
        )
    return cells


def rms_norm(values, gain_row):
    mean_square = jnp.mean(values * values, axis=-1, keepdims=True)
    return values * lax.rsqrt(mean_square + EPSILON) * gain_row


def halo_plan(latents, input_weight, norm_gains, output_weight):
    clip_count = latents.shape[0]
    frames_local = latents.shape[1]
    tile_side = latents.shape[2]
    model_width = latents.shape[4]
    heads_local = input_weight.shape[2]
    head_dim = input_weight.shape[3]
    projected = jnp.einsum(
        "cfhwd,dsne->cfhwsne",
        lax.all_gather(latents, "ta", axis=1, tiled=True),
        input_weight,
        preferred_element_type=jnp.float32,
    )
    query_normed = rms_norm(projected[:, :, :, :, 0], norm_gains[0])
    key_normed = rms_norm(projected[:, :, :, :, 1], norm_gains[1])
    stacked = jnp.stack([query_normed, key_normed, projected[:, :, :, :, 2]], axis=4).astype(
        jnp.bfloat16
    )
    frames = stacked.shape[1]
    query_all = stacked[:, :, :, :, 0]
    key_value = stacked[:, :, :, :, 1:]
    beside_all = padded(key_value, (("ha", 2), ("wa", 3)), tile_side)
    height_index = lax.axis_index("ha")
    width_index = lax.axis_index("wa")
    band_rows = jnp.stack(
        [height_index > 0, height_index >= 0, height_index < lax.axis_size("ha") - 1]
    )
    band_cols = jnp.stack(
        [width_index > 0, width_index >= 0, width_index < lax.axis_size("wa") - 1]
    )
    rows_valid = jnp.repeat(band_rows, tile_side)
    cols_valid = jnp.repeat(band_cols, tile_side)
    around_mask = (rows_valid[:, None] & cols_valid[None, :]).reshape(-1)
    spatial = tile_side * tile_side
    around_len = 9 * spatial
    queries = query_all.reshape(clip_count, frames, spatial, heads_local, head_dim)
    keys_all = beside_all[:, :, :, :, 0].reshape(
        clip_count, frames, around_len, heads_local, head_dim
    )
    values_all = beside_all[:, :, :, :, 1].reshape(
        clip_count, frames, around_len, heads_local, head_dim
    )
    inv_root = 1.0 / math.sqrt(head_dim)
    tile_count = -(-frames // TILE_T)
    pieces = []
    for tile_at in range(tile_count):
        query_low = tile_at * TILE_T
        query_high = min(query_low + TILE_T, frames)
        key_low = max(query_low - TILE_T, 0)
        key_high = min(query_low + 2 * TILE_T, frames)
        query_block = queries[:, query_low:query_high].reshape(
            clip_count, (query_high - query_low) * spatial, heads_local, head_dim
        )
        key_block = keys_all.reshape(
            clip_count, (key_high - key_low) * around_len, heads_local, head_dim
        )
        value_block = values_all.reshape(
            clip_count, (key_high - key_low) * around_len, heads_local, head_dim
        )
        key_mask = jnp.tile(around_mask, key_high - key_low)
        scores = (
            jnp.einsum(
                "cqnd,cknd->ncqk", query_block, key_block, preferred_element_type=jnp.float32
            )
            * inv_root
        )
        scores = jnp.where(key_mask, scores, -1e30)
        row_peak = jnp.max(scores, axis=-1, keepdims=True)
        weights = jnp.exp(scores - row_peak)
        probability = (weights / jnp.sum(weights, axis=-1, keepdims=True)).astype(jnp.bfloat16)
        pieces.append(
            jnp.einsum(
                "ncqk,cknd->ncqd", probability, value_block, preferred_element_type=jnp.float32
            ).astype(jnp.bfloat16)
        )
    attended = jnp.concatenate(pieces, axis=2).reshape(
        heads_local, clip_count, frames, spatial, head_dim
    )
    own_rows = lax.psum_scatter(
        jnp.einsum("ncfqd,nde->fcqe", attended, output_weight, preferred_element_type=jnp.float32),
        "ta",
        scatter_dimension=0,
        tiled=True,
    )
    result = own_rows.transpose(1, 0, 2, 3).reshape(
        clip_count, frames_local, tile_side, tile_side, model_width
    )
    return result.astype(jnp.bfloat16)


MIX_VMEM = 20 << 20
ATTEND_VMEM = 32 << 20


def shift_perm(count, by):
    return [(i, (i + by) % count) for i in range(count)]


def after(value, earlier):
    return lax.optimization_barrier((value, earlier))[0]


def attention_kernel(parts, columns, scale, first, last, scalar_ref, *refs):
    queries = refs[:parts]
    rest = refs[parts:]
    if not first:
        before_refs, rest = rest[:parts], rest[parts:]
    kv_refs, out_ref = rest[:-1], rest[-1]
    groups = len(kv_refs) // 3
    head_dim = queries[0].shape[-1]
    at_peak = 2 * head_dim - 1
    to_exp2 = scale * math.log2(math.e)
    column = pl.program_id(1)
    edge = (column == 0) | (column == columns - 1)
    both = scalar_ref[0] > 0

    def block(start, width, rows):
        query = jnp.concatenate([ref[0, 0] for ref in queries], axis=0)
        keys, values = [], []
        for ref in kv_refs[: rows * groups]:
            tokens = ref.shape[3]
            key = ref[pl.ds(start, width), 0, 0].reshape(width * tokens, head_dim)
            value = ref[pl.ds(start, width), 0, 1].reshape(width * tokens, head_dim)
            keys.append(key)
            values.append(jnp.concatenate([value, jnp.ones_like(value)], axis=1))
        halves = 2
        each = query.shape[0] // halves

        def score(half, key):
            return lax.dot_general(
                query[half * each : (half + 1) * each],
                key,
                (((1,), (1,)), ((), ())),
                preferred_element_type=jnp.float32,
            )

        scores = [score(0, key) for key in keys]
        for half in range(halves):
            here = slice(half * each, (half + 1) * each)
            peak = None
            for part in scores:
                for low in range(0, part.shape[1], head_dim):
                    piece = part[:, low : low + head_dim]
                    peak = piece if peak is None else jnp.maximum(peak, piece)
            peak = peak.max(axis=1, keepdims=True)
            if not first:
                before = jnp.concatenate([ref[0, 0] for ref in before_refs], axis=0)[here]
                old_peak = before[:, at_peak:]
                peak = jnp.maximum(peak, old_peak)
            offset = peak * to_exp2
            summed = None
            ahead = []
            for key, value, part in zip(keys, values, scores):
                if half + 1 < halves:
                    ahead.append(score(half + 1, key))
                weight = jnp.exp2(part * to_exp2 - offset).astype(jnp.bfloat16)
                term = jnp.dot(weight, value, preferred_element_type=jnp.float32)
                summed = term if summed is None else summed + term
            if not first:
                fade = jnp.exp2(old_peak * to_exp2 - offset)
                summed = summed + before * fade
            if last:
                out = summed[:, :head_dim] / summed[:, head_dim : head_dim + 1]
                out = out.astype(out_ref.dtype)
                piece = out_ref.shape[3]
                size = min(piece, each)
                for low in range(0, each, size):
                    place, at = divmod(half * each + low, piece)
                    out_ref[scalar_ref[1 + place], 0, 0, at : at + size] = out[low : low + size]
            else:
                out_ref[0, 0, here, :] = summed
                out_ref[0, 0, here, at_peak:] = peak
            scores = ahead

    for at_edge in (True, False):
        for rows in (2, 3):
            start = jnp.where(column == 0, 0, columns - 2) if at_edge else column - 1
            case = (edge == at_edge) & (both == (rows == 3))
            pl.when(case)(functools.partial(block, start, 2 if at_edge else 3, rows))


def attend(scalars, queries, states, rows, scale, places=0):
    columns, heads, _, head_dim = queries[0].shape
    tokens = sum(query.shape[2] for query in queries)
    keys = sum(kv.shape[3] for kv in rows) * 10 // 4

    def at_query(h, c, v):
        return (c, h, 0, 0)

    def kv_spec(kv):
        return pl.BlockSpec(
            (columns, 1, 2, kv.shape[3], head_dim), lambda h, c, v: (0, h, 0, 0, 0)
        )

    if places:
        each = tokens // places
        out_spec = pl.BlockSpec(
            (places, 1, 1, each, head_dim), lambda h, c, v: (0, c, h, 0, 0)
        )
        out_shape = jax.ShapeDtypeStruct((places, columns, heads, each, head_dim), jnp.bfloat16)
    else:
        out_spec = pl.BlockSpec((1, 1, tokens, 2 * head_dim), at_query)
        out_shape = jax.ShapeDtypeStruct((columns, heads, tokens, 2 * head_dim), jnp.float32)
    pairs = heads * columns * tokens * keys
    arrays = [*queries, *states, *rows]
    in_specs = [
        pl.BlockSpec((1, 1, query.shape[2], head_dim), at_query) for query in queries
    ]
    in_specs += [
        pl.BlockSpec((1, 1, state.shape[2], 2 * head_dim), at_query) for state in states
    ]
    in_specs += [kv_spec(kv) for kv in rows]
    return pl.pallas_call(
        functools.partial(
            attention_kernel, len(queries), columns, scale, not states, bool(places)
        ),
        grid_spec=pltpu.PrefetchScalarGridSpec(
            num_scalar_prefetch=1,
            grid=(heads, columns),
            in_specs=in_specs,
            out_specs=out_spec,
        ),
        out_shape=out_shape,
        cost_estimate=pl.CostEstimate(
            flops=pairs * head_dim * 8, bytes_accessed=pairs * 4, transcendentals=pairs
        ),
        compiler_params=pltpu.CompilerParams(vmem_limit_bytes=ATTEND_VMEM),
        name="tile_attention",
    )(scalars, *arrays)


def mix_kernel(at_ref, attended_ref, *refs):
    weight_refs, out_ref = refs[:-1], refs[-1]
    places = []
    for ref in weight_refs:
        for k in range(ref.shape[0]):
            places.append((ref, k))
    total = 0.0
    for at in range(0, len(places), 2):
        pair = places[at : at + 2]
        left = jnp.concatenate([attended_ref[at_ref[at + i]] for i in range(len(pair))], axis=1)
        right = jnp.concatenate([ref[k] for ref, k in pair], axis=0)
        total = total + jnp.dot(left, right, preferred_element_type=jnp.float32)
    out_ref[...] = total.astype(out_ref.dtype)


def mix(order, attended, weights):
    heads, tokens, head_dim = attended.shape
    width = weights[0].shape[-1]
    step = math.gcd(width, 1024)
    return pl.pallas_call(
        mix_kernel,
        grid_spec=pltpu.PrefetchScalarGridSpec(
            num_scalar_prefetch=1,
            grid=(width // step,),
            in_specs=[pl.BlockSpec(attended.shape, lambda i, o: (0, 0, 0))]
            + [
                pl.BlockSpec((weight.shape[0], head_dim, step), lambda i, o: (0, 0, i))
                for weight in weights
            ],
            out_specs=pl.BlockSpec((tokens, step), lambda i, o: (0, i)),
        ),
        out_shape=jax.ShapeDtypeStruct((tokens, width), jnp.bfloat16),
        cost_estimate=pl.CostEstimate(
            flops=2 * heads * tokens * head_dim * width,
            bytes_accessed=2 * heads * head_dim * width,
            transcendentals=0,
        ),
        compiler_params=pltpu.CompilerParams(vmem_limit_bytes=MIX_VMEM),
        name="mix_heads",
    )(order, attended, *weights)


def row_plan(latents, input_weight, norm_gains, output_weight):
    frame_parts = lax.axis_size("ta")
    row_parts = lax.axis_size("ha")
    col_parts = lax.axis_size("wa")
    heads_local, head_dim = input_weight.shape[2:]
    heads_each = heads_local // col_parts
    here, column_at = lax.axis_index("ta"), lax.axis_index("wa")
    chunks = [latents]
    for by in range(1, frame_parts):
        chunks.append(lax.ppermute(latents, "ta", shift_perm(frame_parts, by)))

    fetched = []
    for by in range(1, frame_parts):
        for mask in range(0, col_parts, 2):
            for k in range(heads_each):
                head = (column_at ^ mask) * heads_each + k
                share = lax.dynamic_slice_in_dim(output_weight, head, 1, axis=0)
                share = lax.ppermute(share, "ta", shift_perm(frame_parts, by))
                fetched.append((by, mask, k, share))

    def project(chunk):
        return jnp.einsum(
            "cfhwd,dsne->cfhwsne", chunk, input_weight, preferred_element_type=jnp.float32
        )

    def as_query(projected):
        query = rms_norm(projected, norm_gains[0]).astype(jnp.bfloat16)
        query = query.transpose(4, 0, 1, 2, 3, 5)
        return query.reshape(col_parts, heads_each, -1, head_dim)

    def as_key_value(projected):
        key = rms_norm(projected[:, :, :, :, 0], norm_gains[1]).astype(jnp.bfloat16)
        value = projected[:, :, :, :, 1].astype(jnp.bfloat16)
        key_value = jnp.stack([key, value]).transpose(5, 0, 1, 2, 3, 4, 6)
        return key_value.reshape(col_parts, heads_each, 2, -1, head_dim)

    queries, keys_values = [], []
    ready = None
    for chunk in chunks:
        if ready is not None:
            chunk = after(chunk, ready)
        projected = project(chunk)
        key_value = as_key_value(projected[:, :, :, :, 1:])
        query = as_query(projected[:, :, :, :, 0])
        ready = (query, key_value)
        keys_values.append(lax.all_to_all(key_value, "wa", 0, 0))
        queries.append(lax.all_to_all(query, "wa", 0, 0))
    pair = [(i, i ^ 1) for i in range(row_parts)]
    side = []
    for i in range(row_parts):
        for k in range(col_parts):
            if 0 < i < row_parts - 1:
                to = (((i + 1) ^ 1) - 1) * col_parts + k
            else:
                to = i * col_parts + (k ^ 1)
            side.append((i * col_parts + k, to))
    rows = []
    for key_value in keys_values:
        paired = lax.ppermute(key_value, "ha", pair)
        beside = lax.ppermute(key_value, ("ha", "wa"), side)
        rows.append((key_value, paired, beside))
    height_index = lax.axis_index("ha")
    inside = (height_index > 0) & (height_index < row_parts - 1)
    places = [lax.rem(here + (frame_parts - by), frame_parts) for by in range(frame_parts)]
    scalars = jnp.stack([inside.astype(jnp.int32)] + places)
    scale = 1.0 / math.sqrt(head_dim)

    states = []
    for query in queries:
        states.append(attend(scalars, [query], [], rows[0], scale))
    last_rows = [row[k] for k in range(3) for row in rows[1:]]
    attended = attend(scalars, queries, states, last_rows, scale, frame_parts)
    sent = attended.reshape(frame_parts * col_parts, heads_each, -1, head_dim)
    got = lax.all_to_all(sent, ("ta", "wa"), 0, 0)
    got = got.reshape(frame_parts * heads_local, -1, head_dim)
    order = [here * heads_local + k for k in range(heads_local)]
    weights = [output_weight]
    swap = [(i, i ^ 1) for i in range(col_parts)]
    for by, mask, k, share in fetched:
        other = lax.ppermute(share, "wa", swap)
        for part, got_mask in ((share, mask), (other, mask ^ 1)):
            weights.append(part)
            order.append(
                places[by] * heads_local + (column_at ^ got_mask) * heads_each + k
            )
    result = mix(jnp.stack(order).astype(jnp.int32), got, weights)
    return result.reshape(latents.shape)


def solution(mesh):
    in_specs = (
        P(None, "ta", "ha", "wa", None),
        P(None, None, "ta", None),
        P(),
        P("ta", None, None),
    )
    out_specs = P(None, "ta", "ha", "wa", None)

    def per_device(latents, input_weight, norm_gains, output_weight):
        frames = latents.shape[1] * lax.axis_size("ta")
        width = lax.axis_size("wa")
        dealt_heads = input_weight.shape[2] % width == 0 and width & (width - 1) == 0
        dealt_heads &= lax.axis_size("ha") % 2 == 0 and lax.axis_size("ta") > 1 and width > 1
        if latents.shape[0] == 1 and dealt_heads and frames <= 2 * TILE_T:
            return row_plan(latents, input_weight, norm_gains, output_weight)
        return halo_plan(latents, input_weight, norm_gains, output_weight)

    return jax.shard_map(
        per_device, mesh=mesh, in_specs=in_specs, out_specs=out_specs, check_vma=False
    )
```

```python
import functools
import math

import jax
import jax.numpy as jnp
from jax import lax
from jax.experimental import pallas as pl
from jax.experimental.pallas import tpu as pltpu
from jax.sharding import PartitionSpec as P


TILE_T = 4


EPSILON = 1e-06


def padded(cells, sides, width):
    for axis, dim in sides:
        count = lax.axis_size(axis)
        ends = count - 1
        head = lax.slice_in_dim(cells, 0, width, axis=dim)
        tail = lax.slice_in_dim(cells, cells.shape[dim] - width, cells.shape[dim], axis=dim)
        cells = jnp.concatenate(
            [
                lax.ppermute(tail, axis, [(i, (i + 1) % count) for i in range(ends)]),
                cells,
                lax.ppermute(head, axis, [((i + 1) % count, i) for i in range(ends)]),
            ],
            axis=dim,
        )
    return cells


def rms_norm(values, gain_row):
    mean_square = jnp.mean(values * values, axis=-1, keepdims=True)
    return values * lax.rsqrt(mean_square + EPSILON) * gain_row


def halo_plan(latents, input_weight, norm_gains, output_weight):
    clip_count = latents.shape[0]
    frames_local = latents.shape[1]
    tile_side = latents.shape[2]
    model_width = latents.shape[4]
    heads_local = input_weight.shape[2]
    head_dim = input_weight.shape[3]
    projected = jnp.einsum(
        "cfhwd,dsne->cfhwsne",
        lax.all_gather(latents, "ta", axis=1, tiled=True),
        input_weight,
        preferred_element_type=jnp.float32,
    )
    query_normed = rms_norm(projected[:, :, :, :, 0], norm_gains[0])
    key_normed = rms_norm(projected[:, :, :, :, 1], norm_gains[1])
    stacked = jnp.stack([query_normed, key_normed, projected[:, :, :, :, 2]], axis=4).astype(
        jnp.bfloat16
    )
    frames = stacked.shape[1]
    query_all = stacked[:, :, :, :, 0]
    key_value = stacked[:, :, :, :, 1:]
    beside_all = padded(key_value, (("ha", 2), ("wa", 3)), tile_side)
    height_index = lax.axis_index("ha")
    width_index = lax.axis_index("wa")
    band_rows = jnp.stack(
        [height_index > 0, height_index >= 0, height_index < lax.axis_size("ha") - 1]
    )
    band_cols = jnp.stack(
        [width_index > 0, width_index >= 0, width_index < lax.axis_size("wa") - 1]
    )
    rows_valid = jnp.repeat(band_rows, tile_side)
    cols_valid = jnp.repeat(band_cols, tile_side)
    around_mask = (rows_valid[:, None] & cols_valid[None, :]).reshape(-1)
    spatial = tile_side * tile_side
    around_len = 9 * spatial
    queries = query_all.reshape(clip_count, frames, spatial, heads_local, head_dim)
    keys_all = beside_all[:, :, :, :, 0].reshape(
        clip_count, frames, around_len, heads_local, head_dim
    )
    values_all = beside_all[:, :, :, :, 1].reshape(
        clip_count, frames, around_len, heads_local, head_dim
    )
    inv_root = 1.0 / math.sqrt(head_dim)
    tile_count = -(-frames // TILE_T)
    pieces = []
    for tile_at in range(tile_count):
        query_low = tile_at * TILE_T
        query_high = min(query_low + TILE_T, frames)
        key_low = max(query_low - TILE_T, 0)
        key_high = min(query_low + 2 * TILE_T, frames)
        query_block = queries[:, query_low:query_high].reshape(
            clip_count, (query_high - query_low) * spatial, heads_local, head_dim
        )
        key_block = keys_all.reshape(
            clip_count, (key_high - key_low) * around_len, heads_local, head_dim
        )
        value_block = values_all.reshape(
            clip_count, (key_high - key_low) * around_len, heads_local, head_dim
        )
        key_mask = jnp.tile(around_mask, key_high - key_low)
        scores = (
            jnp.einsum(
                "cqnd,cknd->ncqk", query_block, key_block, preferred_element_type=jnp.float32
            )
            * inv_root
        )
        scores = jnp.where(key_mask, scores, -1e30)
        row_peak = jnp.max(scores, axis=-1, keepdims=True)
        weights = jnp.exp(scores - row_peak)
        probability = (weights / jnp.sum(weights, axis=-1, keepdims=True)).astype(jnp.bfloat16)
        pieces.append(
            jnp.einsum(
                "ncqk,cknd->ncqd", probability, value_block, preferred_element_type=jnp.float32
            ).astype(jnp.bfloat16)
        )
    attended = jnp.concatenate(pieces, axis=2).reshape(
        heads_local, clip_count, frames, spatial, head_dim
    )
    own_rows = lax.psum_scatter(
        jnp.einsum("ncfqd,nde->fcqe", attended, output_weight, preferred_element_type=jnp.float32),
        "ta",
        scatter_dimension=0,
        tiled=True,
    )
    result = own_rows.transpose(1, 0, 2, 3).reshape(
        clip_count, frames_local, tile_side, tile_side, model_width
    )
    return result.astype(jnp.bfloat16)


MIX_VMEM = 20 << 20
ATTEND_VMEM = 32 << 20


def shift_perm(count, by):
    return [(i, (i + by) % count) for i in range(count)]


def after(value, earlier):
    return lax.optimization_barrier((value, earlier))[0]


def attention_kernel(parts, columns, scale, first, last, scalar_ref, *refs):
    queries = refs[:parts]
    rest = refs[parts:]
    if not first:
        before_refs, rest = rest[:parts], rest[parts:]
    kv_refs, out_ref = rest[:-1], rest[-1]
    groups = len(kv_refs) // 3
    head_dim = queries[0].shape[-1]
    at_peak = 2 * head_dim - 1
    to_exp2 = scale * math.log2(math.e)
    column = pl.program_id(1)
    edge = (column == 0) | (column == columns - 1)
    both = scalar_ref[0] > 0

    def block(start, width, rows):
        query = jnp.concatenate([ref[0, 0] for ref in queries], axis=0)
        keys, values = [], []
        for ref in kv_refs[: rows * groups]:
            tokens = ref.shape[3]
            key = ref[pl.ds(start, width), 0, 0].reshape(width * tokens, head_dim)
            value = ref[pl.ds(start, width), 0, 1].reshape(width * tokens, head_dim)
            keys.append(key)
            values.append(jnp.concatenate([value, jnp.ones_like(value)], axis=1))
        halves = 2
        each = query.shape[0] // halves

        def score(half, key):
            return lax.dot_general(
                query[half * each : (half + 1) * each],
                key,
                (((1,), (1,)), ((), ())),
                preferred_element_type=jnp.float32,
            )

        scores = [score(0, key) for key in keys]
        for half in range(halves):
            here = slice(half * each, (half + 1) * each)
            peak = None
            for part in scores:
                for low in range(0, part.shape[1], head_dim):
                    piece = part[:, low : low + head_dim]
                    peak = piece if peak is None else jnp.maximum(peak, piece)
            peak = peak.max(axis=1, keepdims=True)
            if not first:
                before = jnp.concatenate([ref[0, 0] for ref in before_refs], axis=0)[here]
                old_peak = before[:, at_peak:]
                peak = jnp.maximum(peak, old_peak)
            offset = peak * to_exp2
            summed = None
            ahead = []
            for key, value, part in zip(keys, values, scores):
                if half + 1 < halves:
                    ahead.append(score(half + 1, key))
                weight = jnp.exp2(part * to_exp2 - offset).astype(jnp.bfloat16)
                term = jnp.dot(weight, value, preferred_element_type=jnp.float32)
                summed = term if summed is None else summed + term
            if not first:
                fade = jnp.exp2(old_peak * to_exp2 - offset)
                summed = summed + before * fade
            if last:
                out = summed[:, :head_dim] / summed[:, head_dim : head_dim + 1]
                out = out.astype(out_ref.dtype)
                piece = out_ref.shape[3]
                size = min(piece, each)
                for low in range(0, each, size):
                    place, at = divmod(half * each + low, piece)
                    out_ref[scalar_ref[1 + place], 0, 0, at : at + size] = out[low : low + size]
            else:
                out_ref[0, 0, here, :] = summed
                out_ref[0, 0, here, at_peak:] = peak
            scores = ahead

    for at_edge in (True, False):
        for rows in (2, 3):
            start = jnp.where(column == 0, 0, columns - 2) if at_edge else column - 1
            case = (edge == at_edge) & (both == (rows == 3))
            pl.when(case)(functools.partial(block, start, 2 if at_edge else 3, rows))


def attend(scalars, queries, states, rows, scale, places=0):
    columns, heads, _, head_dim = queries[0].shape
    tokens = sum(query.shape[2] for query in queries)
    keys = sum(kv.shape[3] for kv in rows) * 10 // 4

    def at_query(h, c, v):
        return (c, h, 0, 0)

    def kv_spec(kv):
        return pl.BlockSpec(
            (columns, 1, 2, kv.shape[3], head_dim), lambda h, c, v: (0, h, 0, 0, 0)
        )

    if places:
        each = tokens // places
        out_spec = pl.BlockSpec(
            (places, 1, 1, each, head_dim), lambda h, c, v: (0, c, h, 0, 0)
        )
        out_shape = jax.ShapeDtypeStruct((places, columns, heads, each, head_dim), jnp.bfloat16)
    else:
        out_spec = pl.BlockSpec((1, 1, tokens, 2 * head_dim), at_query)
        out_shape = jax.ShapeDtypeStruct((columns, heads, tokens, 2 * head_dim), jnp.float32)
    pairs = heads * columns * tokens * keys
    arrays = [*queries, *states, *rows]
    in_specs = [
        pl.BlockSpec((1, 1, query.shape[2], head_dim), at_query) for query in queries
    ]
    in_specs += [
        pl.BlockSpec((1, 1, state.shape[2], 2 * head_dim), at_query) for state in states
    ]
    in_specs += [kv_spec(kv) for kv in rows]
    return pl.pallas_call(
        functools.partial(
            attention_kernel, len(queries), columns, scale, not states, bool(places)
        ),
        grid_spec=pltpu.PrefetchScalarGridSpec(
            num_scalar_prefetch=1,
            grid=(heads, columns),
            in_specs=in_specs,
            out_specs=out_spec,
        ),
        out_shape=out_shape,
        cost_estimate=pl.CostEstimate(
            flops=pairs * head_dim * 8, bytes_accessed=pairs * 4, transcendentals=pairs
        ),
        compiler_params=pltpu.CompilerParams(vmem_limit_bytes=ATTEND_VMEM),
        name="tile_attention",
    )(scalars, *arrays)


def mix_kernel(at_ref, attended_ref, *refs):
    weight_refs, out_ref = refs[:-1], refs[-1]
    places = []
    for ref in weight_refs:
        for k in range(ref.shape[0]):
            places.append((ref, k))
    total = 0.0
    for at in range(0, len(places), 2):
        pair = places[at : at + 2]
        left = jnp.concatenate([attended_ref[at_ref[at + i]] for i in range(len(pair))], axis=1)
        right = jnp.concatenate([ref[k] for ref, k in pair], axis=0)
        total = total + jnp.dot(left, right, preferred_element_type=jnp.float32)
    out_ref[...] = total.astype(out_ref.dtype)


def mix(order, attended, weights):
    heads, tokens, head_dim = attended.shape
    width = weights[0].shape[-1]
    step = math.gcd(width, 1024)
    return pl.pallas_call(
        mix_kernel,
        grid_spec=pltpu.PrefetchScalarGridSpec(
            num_scalar_prefetch=1,
            grid=(width // step,),
            in_specs=[pl.BlockSpec(attended.shape, lambda i, o: (0, 0, 0))]
            + [
                pl.BlockSpec((weight.shape[0], head_dim, step), lambda i, o: (0, 0, i))
                for weight in weights
            ],
            out_specs=pl.BlockSpec((tokens, step), lambda i, o: (0, i)),
        ),
        out_shape=jax.ShapeDtypeStruct((tokens, width), jnp.bfloat16),
        cost_estimate=pl.CostEstimate(
            flops=2 * heads * tokens * head_dim * width,
            bytes_accessed=2 * heads * head_dim * width,
            transcendentals=0,
        ),
        compiler_params=pltpu.CompilerParams(vmem_limit_bytes=MIX_VMEM),
        name="mix_heads",
    )(order, attended, *weights)


def row_plan(latents, input_weight, norm_gains, output_weight):
    frame_parts = lax.axis_size("ta")
    row_parts = lax.axis_size("ha")
    col_parts = lax.axis_size("wa")
    heads_local, head_dim = input_weight.shape[2:]
    heads_each = heads_local // col_parts
    here, column_at = lax.axis_index("ta"), lax.axis_index("wa")
    chunks = [latents]
    for by in range(1, frame_parts):
        chunks.append(lax.ppermute(latents, "ta", shift_perm(frame_parts, by)))

    fetched = []
    for by in range(1, frame_parts):
        for mask in range(0, col_parts, 2):
            for k in range(heads_each):
                head = (column_at ^ mask) * heads_each + k
                share = lax.dynamic_slice_in_dim(output_weight, head, 1, axis=0)
                share = lax.ppermute(share, "ta", shift_perm(frame_parts, by))
                fetched.append((by, mask, k, share))

    def project(chunk):
        return jnp.einsum(
            "cfhwd,dsne->cfhwsne", chunk, input_weight, preferred_element_type=jnp.float32
        )

    def as_query(projected):
        query = rms_norm(projected, norm_gains[0]).astype(jnp.bfloat16)
        query = query.transpose(4, 0, 1, 2, 3, 5)
        return query.reshape(col_parts, heads_each, -1, head_dim)

    def as_key_value(projected):
        key = rms_norm(projected[:, :, :, :, 0], norm_gains[1]).astype(jnp.bfloat16)
        value = projected[:, :, :, :, 1].astype(jnp.bfloat16)
        halves = [
            half.transpose(4, 0, 1, 2, 3, 5).reshape(col_parts, heads_each, 1, -1, head_dim)
            for half in (key, value)
        ]
        return jnp.concatenate(halves, axis=2)

    queries, keys_values = [], []
    ready = None
    for chunk in chunks:
        if ready is not None:
            chunk = after(chunk, ready)
        projected = project(chunk)
        key_value = as_key_value(projected[:, :, :, :, 1:])
        query = as_query(projected[:, :, :, :, 0])
        ready = (query, key_value)
        dealt = lax.all_to_all(key_value, "wa", 0, 0)
        keys_values.append(after(dealt, query))
        queries.append(lax.all_to_all(query, "wa", 0, 0))
    pair = [(i, i ^ 1) for i in range(row_parts)]
    side = []
    for i in range(row_parts):
        for k in range(col_parts):
            if 0 < i < row_parts - 1:
                to = (((i + 1) ^ 1) - 1) * col_parts + k
            else:
                to = i * col_parts + (k ^ 1)
            side.append((i * col_parts + k, to))
    rows = []
    for key_value in keys_values:
        paired = lax.ppermute(key_value, "ha", pair)
        beside = lax.ppermute(key_value, ("ha", "wa"), side)
        rows.append((key_value, paired, beside))
    height_index = lax.axis_index("ha")
    inside = (height_index > 0) & (height_index < row_parts - 1)
    places = [lax.rem(here + (frame_parts - by), frame_parts) for by in range(frame_parts)]
    scalars = jnp.stack([inside.astype(jnp.int32)] + places)
    scale = 1.0 / math.sqrt(head_dim)

    states = []
    for query in queries:
        states.append(attend(scalars, [query], [], rows[0], scale))
    last_rows = [row[k] for k in range(3) for row in rows[1:]]
    attended = attend(scalars, queries, states, last_rows, scale, frame_parts)
    sent = attended.reshape(frame_parts * col_parts, heads_each, -1, head_dim)
    got = lax.all_to_all(sent, ("ta", "wa"), 0, 0)
    got = got.reshape(frame_parts * heads_local, -1, head_dim)
    order = [here * heads_local + k for k in range(heads_local)]
    weights = [output_weight]
    swap = [(i, i ^ 1) for i in range(col_parts)]
    for by, mask, k, share in fetched:
        other = lax.ppermute(share, "wa", swap)
        for part, got_mask in ((share, mask), (other, mask ^ 1)):
            weights.append(part)
            order.append(
                places[by] * heads_local + (column_at ^ got_mask) * heads_each + k
            )
    result = mix(jnp.stack(order).astype(jnp.int32), got, weights)
    return result.reshape(latents.shape)


def solution(mesh):
    in_specs = (
        P(None, "ta", "ha", "wa", None),
        P(None, None, "ta", None),
        P(),
        P("ta", None, None),
    )
    out_specs = P(None, "ta", "ha", "wa", None)

    def per_device(latents, input_weight, norm_gains, output_weight):
        frames = latents.shape[1] * lax.axis_size("ta")
        width = lax.axis_size("wa")
        dealt_heads = input_weight.shape[2] % width == 0 and width & (width - 1) == 0
        dealt_heads &= lax.axis_size("ha") % 2 == 0 and lax.axis_size("ta") > 1 and width > 1
        if latents.shape[0] == 1 and dealt_heads and frames <= 2 * TILE_T:
            return row_plan(latents, input_weight, norm_gains, output_weight)
        return halo_plan(latents, input_weight, norm_gains, output_weight)

    return jax.shard_map(
        per_device, mesh=mesh, in_specs=in_specs, out_specs=out_specs, check_vma=False
    )
```

```python
import functools
import math

import jax
import jax.numpy as jnp
from jax import lax
from jax.experimental import pallas as pl
from jax.experimental.pallas import tpu as pltpu
from jax.sharding import PartitionSpec as P


TILE_T = 4


EPSILON = 1e-06


def padded(cells, sides, width):
    for axis, dim in sides:
        count = lax.axis_size(axis)
        ends = count - 1
        head = lax.slice_in_dim(cells, 0, width, axis=dim)
        tail = lax.slice_in_dim(cells, cells.shape[dim] - width, cells.shape[dim], axis=dim)
        cells = jnp.concatenate(
            [
                lax.ppermute(tail, axis, [(i, (i + 1) % count) for i in range(ends)]),
                cells,
                lax.ppermute(head, axis, [((i + 1) % count, i) for i in range(ends)]),
            ],
            axis=dim,
        )
    return cells


def rms_norm(values, gain_row):
    mean_square = jnp.mean(values * values, axis=-1, keepdims=True)
    return values * lax.rsqrt(mean_square + EPSILON) * gain_row


def halo_plan(latents, input_weight, norm_gains, output_weight):
    clip_count = latents.shape[0]
    frames_local = latents.shape[1]
    tile_side = latents.shape[2]
    model_width = latents.shape[4]
    heads_local = input_weight.shape[2]
    head_dim = input_weight.shape[3]
    projected = jnp.einsum(
        "cfhwd,dsne->cfhwsne",
        lax.all_gather(latents, "ta", axis=1, tiled=True),
        input_weight,
        preferred_element_type=jnp.float32,
    )
    query_normed = rms_norm(projected[:, :, :, :, 0], norm_gains[0])
    key_normed = rms_norm(projected[:, :, :, :, 1], norm_gains[1])
    stacked = jnp.stack([query_normed, key_normed, projected[:, :, :, :, 2]], axis=4).astype(
        jnp.bfloat16
    )
    frames = stacked.shape[1]
    query_all = stacked[:, :, :, :, 0]
    key_value = stacked[:, :, :, :, 1:]
    beside_all = padded(key_value, (("ha", 2), ("wa", 3)), tile_side)
    height_index = lax.axis_index("ha")
    width_index = lax.axis_index("wa")
    band_rows = jnp.stack(
        [height_index > 0, height_index >= 0, height_index < lax.axis_size("ha") - 1]
    )
    band_cols = jnp.stack(
        [width_index > 0, width_index >= 0, width_index < lax.axis_size("wa") - 1]
    )
    rows_valid = jnp.repeat(band_rows, tile_side)
    cols_valid = jnp.repeat(band_cols, tile_side)
    around_mask = (rows_valid[:, None] & cols_valid[None, :]).reshape(-1)
    spatial = tile_side * tile_side
    around_len = 9 * spatial
    queries = query_all.reshape(clip_count, frames, spatial, heads_local, head_dim)
    keys_all = beside_all[:, :, :, :, 0].reshape(
        clip_count, frames, around_len, heads_local, head_dim
    )
    values_all = beside_all[:, :, :, :, 1].reshape(
        clip_count, frames, around_len, heads_local, head_dim
    )
    inv_root = 1.0 / math.sqrt(head_dim)
    tile_count = -(-frames // TILE_T)
    pieces = []
    for tile_at in range(tile_count):
        query_low = tile_at * TILE_T
        query_high = min(query_low + TILE_T, frames)
        key_low = max(query_low - TILE_T, 0)
        key_high = min(query_low + 2 * TILE_T, frames)
        query_block = queries[:, query_low:query_high].reshape(
            clip_count, (query_high - query_low) * spatial, heads_local, head_dim
        )
        key_block = keys_all.reshape(
            clip_count, (key_high - key_low) * around_len, heads_local, head_dim
        )
        value_block = values_all.reshape(
            clip_count, (key_high - key_low) * around_len, heads_local, head_dim
        )
        key_mask = jnp.tile(around_mask, key_high - key_low)
        scores = (
            jnp.einsum(
                "cqnd,cknd->ncqk", query_block, key_block, preferred_element_type=jnp.float32
            )
            * inv_root
        )
        scores = jnp.where(key_mask, scores, -1e30)
        row_peak = jnp.max(scores, axis=-1, keepdims=True)
        weights = jnp.exp(scores - row_peak)
        probability = (weights / jnp.sum(weights, axis=-1, keepdims=True)).astype(jnp.bfloat16)
        pieces.append(
            jnp.einsum(
                "ncqk,cknd->ncqd", probability, value_block, preferred_element_type=jnp.float32
            ).astype(jnp.bfloat16)
        )
    attended = jnp.concatenate(pieces, axis=2).reshape(
        heads_local, clip_count, frames, spatial, head_dim
    )
    own_rows = lax.psum_scatter(
        jnp.einsum("ncfqd,nde->fcqe", attended, output_weight, preferred_element_type=jnp.float32),
        "ta",
        scatter_dimension=0,
        tiled=True,
    )
    result = own_rows.transpose(1, 0, 2, 3).reshape(
        clip_count, frames_local, tile_side, tile_side, model_width
    )
    return result.astype(jnp.bfloat16)


SMALL_VMEM = 32 << 20
LARGE_VMEM = 60 << 20


def shift_perm(count, by):
    return [(i, (i + by) % count) for i in range(count)]


def after(value, earlier):
    return lax.optimization_barrier((value, earlier))[0]


def attention_kernel(parts, columns, scale, first, last, scalar_ref, *refs):
    queries = refs[:parts]
    rest = refs[parts:]
    if not first:
        before_refs, rest = rest[:parts], rest[parts:]
    kv_refs, out_ref = rest[:-1], rest[-1]
    groups = len(kv_refs) // 3
    head_dim = queries[0].shape[-1]
    at_peak = 2 * head_dim - 1
    to_exp2 = scale * math.log2(math.e)
    column = pl.program_id(1)
    edge = (column == 0) | (column == columns - 1)
    both = scalar_ref[0] > 0

    def block(start, width, rows):
        query = jnp.concatenate([ref[0, 0] for ref in queries], axis=0)
        keys, values = [], []
        for ref in kv_refs[: rows * groups]:
            tokens = ref.shape[3]
            key = ref[pl.ds(start, width), 0, 0].reshape(width * tokens, head_dim)
            value = ref[pl.ds(start, width), 0, 1].reshape(width * tokens, head_dim)
            keys.append(key)
            values.append(jnp.concatenate([value, jnp.ones_like(value)], axis=1))
        halves = 2
        each = query.shape[0] // halves

        def score(half, key):
            return lax.dot_general(
                query[half * each : (half + 1) * each],
                key,
                (((1,), (1,)), ((), ())),
                preferred_element_type=jnp.float32,
            )

        scores = [score(0, key) for key in keys]
        for half in range(halves):
            here = slice(half * each, (half + 1) * each)
            peak = None
            for part in scores:
                for low in range(0, part.shape[1], head_dim):
                    piece = part[:, low : low + head_dim]
                    peak = piece if peak is None else jnp.maximum(peak, piece)
            peak = peak.max(axis=1, keepdims=True)
            if not first:
                before = jnp.concatenate([ref[0, 0] for ref in before_refs], axis=0)[here]
                old_peak = before[:, at_peak:]
                peak = jnp.maximum(peak, old_peak)
            offset = peak * to_exp2
            summed = None
            ahead = []
            for key, value, part in zip(keys, values, scores):
                if half + 1 < halves:
                    ahead.append(score(half + 1, key))
                weight = jnp.exp2(part * to_exp2 - offset).astype(jnp.bfloat16)
                term = jnp.dot(weight, value, preferred_element_type=jnp.float32)
                summed = term if summed is None else summed + term
            if not first:
                fade = jnp.exp2(old_peak * to_exp2 - offset)
                summed = summed + before * fade
            if last:
                out = summed[:, :head_dim] / summed[:, head_dim : head_dim + 1]
                out = out.astype(out_ref.dtype)
                piece = out_ref.shape[3]
                size = min(piece, each)
                for low in range(0, each, size):
                    place, at = divmod(half * each + low, piece)
                    out_ref[scalar_ref[1 + place], 0, 0, at : at + size] = out[low : low + size]
            else:
                out_ref[0, 0, here, :] = summed
                out_ref[0, 0, here, at_peak:] = peak
            scores = ahead

    for at_edge in (True, False):
        for rows in (2, 3):
            start = jnp.where(column == 0, 0, columns - 2) if at_edge else column - 1
            case = (edge == at_edge) & (both == (rows == 3))
            pl.when(case)(functools.partial(block, start, 2 if at_edge else 3, rows))


def attend(scalars, queries, states, rows, scale, places=0, head=None):
    columns, heads, _, head_dim = queries[0].shape
    tokens = sum(query.shape[2] for query in queries)
    keys = sum(kv.shape[3] for kv in rows) * 10 // 4
    low, count = (0, heads) if head is None else (head, 1)

    def at_head(h, low):
        return h + low if low else h

    def at_slot(h, c, v):
        return (c ^ v[v.shape[0] - 1], at_head(h, low), 0, 0)

    def at_query(h, c, v):
        return (c, at_head(h, low), 0, 0)

    def kv_spec(kv):
        start = low if kv.shape[1] == heads else 0
        return pl.BlockSpec(
            (columns, 1, 2, kv.shape[3], head_dim),
            lambda h, c, v: (0, at_head(h, start), 0, 0, 0),
        )

    if places:
        each = tokens // places
        out_spec = pl.BlockSpec(
            (places, 1, 1, each, head_dim), lambda h, c, v: (0, c, h, 0, 0)
        )
        out_shape = jax.ShapeDtypeStruct((places, columns, count, each, head_dim), jnp.bfloat16)
    else:
        out_spec = pl.BlockSpec((1, 1, tokens, 2 * head_dim), at_query)
        out_shape = jax.ShapeDtypeStruct((columns, heads, tokens, 2 * head_dim), jnp.float32)
    pairs = count * columns * tokens * keys
    arrays = [*queries, *states, *rows]
    in_specs = [
        pl.BlockSpec((1, 1, query.shape[2], head_dim), at_slot) for query in queries
    ]
    in_specs += [
        pl.BlockSpec((1, 1, state.shape[2], 2 * head_dim), at_query) for state in states
    ]
    in_specs += [kv_spec(kv) for kv in rows]
    return pl.pallas_call(
        functools.partial(
            attention_kernel, len(queries), columns, scale, not states, bool(places)
        ),
        grid_spec=pltpu.PrefetchScalarGridSpec(
            num_scalar_prefetch=1,
            grid=(count, columns),
            in_specs=in_specs,
            out_specs=out_spec,
        ),
        out_shape=out_shape,
        cost_estimate=pl.CostEstimate(
            flops=pairs * head_dim * 8, bytes_accessed=pairs * 4, transcendentals=pairs
        ),
        compiler_params=pltpu.CompilerParams(vmem_limit_bytes=LARGE_VMEM if head else SMALL_VMEM),
        name="tile_attention",
    )(scalars, *arrays)


def mix_kernel(final, at_ref, attended_ref, *refs):
    out_ref = refs[-1]
    weight_refs = refs[: -2 if final else -1]
    total = refs[-2][...] if final else 0.0
    places = [(ref, k) for ref in weight_refs for k in range(ref.shape[0])]
    for at in range(0, len(places), 2):
        pair = places[at : at + 2]
        left = jnp.concatenate([attended_ref[at_ref[at + i]] for i in range(len(pair))], axis=1)
        right = jnp.concatenate(
            [ref[k].reshape(ref.shape[-2:]) for ref, k in pair], axis=0
        )
        total = total + jnp.dot(left, right, preferred_element_type=jnp.float32)
    out_ref[...] = total.astype(out_ref.dtype)


def mix(order, attended, local, head, weights, total, final):
    _, tokens, head_dim = attended.shape
    width = local.shape[-1]
    step = math.gcd(width, 1024)
    heads = local.shape[0] + len(weights)
    out_spec = pl.BlockSpec((tokens, step), lambda i, o: (0, i))
    final_args = [total] if final else []
    return pl.pallas_call(
        functools.partial(mix_kernel, final),
        grid_spec=pltpu.PrefetchScalarGridSpec(
            num_scalar_prefetch=1,
            grid=(width // step,),
            in_specs=[
                pl.BlockSpec(attended.shape, lambda i, o: (0, 0, 0)),
                pl.BlockSpec((local.shape[0], 1, head_dim, step), lambda i, o: (0, head, 0, i)),
            ]
            + [pl.BlockSpec((1, head_dim, step), lambda i, o: (0, 0, i)) for _ in weights]
            + [out_spec for _ in final_args],
            out_specs=out_spec,
        ),
        out_shape=jax.ShapeDtypeStruct((tokens, width), jnp.bfloat16 if final else jnp.float32),
        cost_estimate=pl.CostEstimate(
            flops=2 * heads * tokens * head_dim * width,
            bytes_accessed=2 * heads * head_dim * width,
            transcendentals=0,
        ),
        compiler_params=pltpu.CompilerParams(vmem_limit_bytes=LARGE_VMEM),
        name="mix_heads",
    )(order, attended, local, *weights, *final_args)


def row_plan(latents, input_weight, norm_gains, output_weight):
    frame_parts = lax.axis_size("ta")
    row_parts = lax.axis_size("ha")
    col_parts = lax.axis_size("wa")
    heads_local, head_dim = input_weight.shape[2:]
    heads_each = heads_local // col_parts
    here, column_at = lax.axis_index("ta"), lax.axis_index("wa")
    chunks = [latents]
    for by in range(1, frame_parts):
        chunks.append(lax.ppermute(latents, "ta", shift_perm(frame_parts, by)))

    fetched = []
    for by in range(1, frame_parts):
        for mask in range(0, col_parts, 2):
            for k in range(heads_each):
                if mask and (mask, k) == (col_parts - 2, heads_each - 1):
                    continue
                head = (column_at ^ mask) * heads_each + k
                share = lax.dynamic_slice_in_dim(output_weight, head, 1, axis=0)
                share = lax.ppermute(share, "ta", shift_perm(frame_parts, by))
                fetched.append((by, mask, k, share))

    for by, mask, k, share in list(fetched):
        if col_parts > 2 and (mask, k) == (0, heads_each - 1):
            mask = col_parts - 2
            share = lax.ppermute(share, "wa", [(i, i ^ mask) for i in range(col_parts)])
            fetched.append((by, mask, k, share))

    def project(chunk):
        return jnp.einsum(
            "cfhwd,dsne->cfhwsne", chunk, input_weight, preferred_element_type=jnp.float32
        )

    def as_query(projected):
        query = rms_norm(projected, norm_gains[0]).astype(jnp.bfloat16)
        query = query.transpose(4, 0, 1, 2, 3, 5)
        return query.reshape(col_parts, heads_each, -1, head_dim)

    def as_key_value(projected):
        key = rms_norm(projected[:, :, :, :, 0], norm_gains[1]).astype(jnp.bfloat16)
        value = projected[:, :, :, :, 1].astype(jnp.bfloat16)
        halves = [
            half.transpose(4, 0, 1, 2, 3, 5).reshape(col_parts, heads_each, 1, -1, head_dim)
            for half in (key, value)
        ]
        return jnp.concatenate(halves, axis=2)

    queries, keys_values = [], []
    ready = None
    for chunk in chunks:
        if ready is not None:
            chunk = after(chunk, ready)
        projected = project(chunk)
        key_value = as_key_value(projected[:, :, :, :, 1:])
        query = as_query(projected[:, :, :, :, 0])
        ready = (query, key_value)
        dealt = lax.all_to_all(key_value, "wa", 0, 0)
        keys_values.append(after(dealt, query))
        slots = [lax.dynamic_index_in_dim(query, column_at, 0, keepdims=False)]
        for by in range(1, col_parts):
            block = lax.dynamic_index_in_dim(query, column_at ^ by, 0, keepdims=False)
            slots.append(lax.ppermute(block, "wa", [(i, i ^ by) for i in range(col_parts)]))
        queries.append(jnp.stack(slots))
    pair = [(i, i ^ 1) for i in range(row_parts)]
    side = []
    for i in range(row_parts):
        for k in range(col_parts):
            if 0 < i < row_parts - 1:
                to = (((i + 1) ^ 1) - 1) * col_parts + k
            else:
                to = i * col_parts + (k ^ 1)
            side.append((i * col_parts + k, to))
    rows = []
    for at, key_value in enumerate(keys_values):
        shares = [key_value]
        if at:
            shares = [key_value[:, head : head + 1] for head in range(heads_each)]
        paired, beside = [], []
        for head, share in enumerate(shares):
            paired.append(lax.ppermute(share, "ha", pair))
            beside.append(lax.ppermute(share, ("ha", "wa"), side))
        rows.append((key_value, paired, beside))
    height_index = lax.axis_index("ha")
    inside = (height_index > 0) & (height_index < row_parts - 1)
    places = [lax.rem(here + (frame_parts - by), frame_parts) for by in range(frame_parts)]
    scalars = jnp.stack([inside.astype(jnp.int32)] + places + [column_at])
    scale = 1.0 / math.sqrt(head_dim)

    first_rows = [rows[0][0], *rows[0][1], *rows[0][2]]
    states = []
    for query in queries:
        states.append(attend(scalars, [query], [], first_rows, scale))

    swap = [(i, i ^ 1) for i in range(col_parts)]
    spread = []
    for by, mask, k, share in fetched:
        other = lax.ppermute(share, "wa", swap)
        spread.append((by, mask, k, share))
        spread.append((by, mask ^ 1, k, other))
    local = output_weight.reshape(col_parts, heads_each, head_dim, -1)
    total = None
    for head in range(heads_each):
        last_rows = [row[0] for row in rows[1:]]
        last_rows += [row[1][head] for row in rows[1:]] + [row[2][head] for row in rows[1:]]
        attended = attend(scalars, queries, states, last_rows, scale, frame_parts, head)
        sent = attended.reshape(frame_parts * col_parts, -1, head_dim)
        got = lax.all_to_all(sent, ("ta", "wa"), 0, 0, tiled=True)
        got = got.reshape(frame_parts * col_parts, -1, head_dim)
        order = [here * col_parts + k for k in range(col_parts)]
        weights = []
        for by, mask, k, part in spread:
            if k == head:
                weights.append(part)
                order.append(places[by] * col_parts + (column_at ^ mask))
        order = jnp.stack(order).astype(jnp.int32)
        total = mix(order, got, local, head, weights, total, head == heads_each - 1)
    return total.reshape(latents.shape)


def solution(mesh):
    in_specs = (
        P(None, "ta", "ha", "wa", None),
        P(None, None, "ta", None),
        P(),
        P("ta", None, None),
    )
    out_specs = P(None, "ta", "ha", "wa", None)

    def per_device(latents, input_weight, norm_gains, output_weight):
        frames = latents.shape[1] * lax.axis_size("ta")
        width = lax.axis_size("wa")
        dealt_heads = input_weight.shape[2] % width == 0 and width & (width - 1) == 0
        dealt_heads &= lax.axis_size("ha") % 2 == 0 and lax.axis_size("ta") > 1 and width > 1
        if latents.shape[0] == 1 and dealt_heads and frames <= 2 * TILE_T:
            return row_plan(latents, input_weight, norm_gains, output_weight)
        return halo_plan(latents, input_weight, norm_gains, output_weight)

    return jax.shard_map(
        per_device, mesh=mesh, in_specs=in_specs, out_specs=out_specs, check_vma=False
    )
```

```python
import functools
import math

import jax
import jax.numpy as jnp
from jax import lax
from jax.experimental import pallas as pl
from jax.experimental.pallas import tpu as pltpu
from jax.sharding import PartitionSpec as P


TILE_T = 4


EPSILON = 1e-06


def padded(cells, sides, width):
    for axis, dim in sides:
        count = lax.axis_size(axis)
        ends = count - 1
        head = lax.slice_in_dim(cells, 0, width, axis=dim)
        tail = lax.slice_in_dim(cells, cells.shape[dim] - width, cells.shape[dim], axis=dim)
        cells = jnp.concatenate(
            [
                lax.ppermute(tail, axis, [(i, (i + 1) % count) for i in range(ends)]),
                cells,
                lax.ppermute(head, axis, [((i + 1) % count, i) for i in range(ends)]),
            ],
            axis=dim,
        )
    return cells


def rms_norm(values, gain_row):
    mean_square = jnp.mean(values * values, axis=-1, keepdims=True)
    return values * lax.rsqrt(mean_square + EPSILON) * gain_row


def halo_plan(latents, input_weight, norm_gains, output_weight):
    clip_count = latents.shape[0]
    frames_local = latents.shape[1]
    tile_side = latents.shape[2]
    model_width = latents.shape[4]
    heads_local = input_weight.shape[2]
    head_dim = input_weight.shape[3]
    projected = jnp.einsum(
        "cfhwd,dsne->cfhwsne",
        lax.all_gather(latents, "ta", axis=1, tiled=True),
        input_weight,
        preferred_element_type=jnp.float32,
    )
    query_normed = rms_norm(projected[:, :, :, :, 0], norm_gains[0])
    key_normed = rms_norm(projected[:, :, :, :, 1], norm_gains[1])
    stacked = jnp.stack([query_normed, key_normed, projected[:, :, :, :, 2]], axis=4).astype(
        jnp.bfloat16
    )
    frames = stacked.shape[1]
    query_all = stacked[:, :, :, :, 0]
    key_value = stacked[:, :, :, :, 1:]
    beside_all = padded(key_value, (("ha", 2), ("wa", 3)), tile_side)
    height_index = lax.axis_index("ha")
    width_index = lax.axis_index("wa")
    band_rows = jnp.stack(
        [height_index > 0, height_index >= 0, height_index < lax.axis_size("ha") - 1]
    )
    band_cols = jnp.stack(
        [width_index > 0, width_index >= 0, width_index < lax.axis_size("wa") - 1]
    )
    rows_valid = jnp.repeat(band_rows, tile_side)
    cols_valid = jnp.repeat(band_cols, tile_side)
    around_mask = (rows_valid[:, None] & cols_valid[None, :]).reshape(-1)
    spatial = tile_side * tile_side
    around_len = 9 * spatial
    queries = query_all.reshape(clip_count, frames, spatial, heads_local, head_dim)
    keys_all = beside_all[:, :, :, :, 0].reshape(
        clip_count, frames, around_len, heads_local, head_dim
    )
    values_all = beside_all[:, :, :, :, 1].reshape(
        clip_count, frames, around_len, heads_local, head_dim
    )
    inv_root = 1.0 / math.sqrt(head_dim)
    tile_count = -(-frames // TILE_T)
    pieces = []
    for tile_at in range(tile_count):
        query_low = tile_at * TILE_T
        query_high = min(query_low + TILE_T, frames)
        key_low = max(query_low - TILE_T, 0)
        key_high = min(query_low + 2 * TILE_T, frames)
        query_block = queries[:, query_low:query_high].reshape(
            clip_count, (query_high - query_low) * spatial, heads_local, head_dim
        )
        key_block = keys_all.reshape(
            clip_count, (key_high - key_low) * around_len, heads_local, head_dim
        )
        value_block = values_all.reshape(
            clip_count, (key_high - key_low) * around_len, heads_local, head_dim
        )
        key_mask = jnp.tile(around_mask, key_high - key_low)
        scores = (
            jnp.einsum(
                "cqnd,cknd->ncqk", query_block, key_block, preferred_element_type=jnp.float32
            )
            * inv_root
        )
        scores = jnp.where(key_mask, scores, -1e30)
        row_peak = jnp.max(scores, axis=-1, keepdims=True)
        weights = jnp.exp(scores - row_peak)
        probability = (weights / jnp.sum(weights, axis=-1, keepdims=True)).astype(jnp.bfloat16)
        pieces.append(
            jnp.einsum(
                "ncqk,cknd->ncqd", probability, value_block, preferred_element_type=jnp.float32
            ).astype(jnp.bfloat16)
        )
    attended = jnp.concatenate(pieces, axis=2).reshape(
        heads_local, clip_count, frames, spatial, head_dim
    )
    own_rows = lax.psum_scatter(
        jnp.einsum("ncfqd,nde->fcqe", attended, output_weight, preferred_element_type=jnp.float32),
        "ta",
        scatter_dimension=0,
        tiled=True,
    )
    result = own_rows.transpose(1, 0, 2, 3).reshape(
        clip_count, frames_local, tile_side, tile_side, model_width
    )
    return result.astype(jnp.bfloat16)


UNIT_ROWS = 256
SMALL_VMEM = 32 << 20
LARGE_VMEM = 60 << 20
MIX_VMEM = 44 << 20


def shift_perm(count, by):
    return [(i, (i + by) % count) for i in range(count)]


def after(value, earlier):
    return lax.optimization_barrier((value, earlier))[0]


def attention_kernel(parts, columns, scale, first, last, scalar_ref, *refs):
    queries = refs[:parts]
    rest = refs[parts:]
    if not first:
        before_refs, rest = rest[:parts], rest[parts:]
    kv_refs, out_ref = rest[:-1], rest[-1]
    groups = len(kv_refs) // 3
    head_dim = queries[0].shape[-1]
    total_rows = sum(ref.shape[2] for ref in queries)
    each = math.gcd(total_rows, UNIT_ROWS)
    at_peak = 2 * head_dim - 1
    to_exp2 = scale * math.log2(math.e)
    pair = pl.program_id(1)
    both = scalar_ref[0] > 0
    odd = scalar_ref[scalar_ref.shape[0] - 1] & 1

    def block(spans, rows):
        keys, values, rows_of = [], [], []
        for at, (start, width) in enumerate(spans):
            keys.append([])
            values.append([])
            for ref in kv_refs[: rows * groups]:
                tokens = ref.shape[3]
                key = ref[pl.ds(start, width), 0, 0].reshape(width * tokens, head_dim)
                value = ref[pl.ds(start, width), 0, 1].reshape(width * tokens, head_dim)
                keys[at].append(key)
                values[at].append(jnp.concatenate([value, jnp.ones_like(value)], axis=1))
            rows_of.append(jnp.concatenate([ref[at ^ odd, 0] for ref in queries], axis=0))
        units = [(at, low) for at in range(2) for low in range(0, total_rows, each)]

        def score(unit, key):
            at, low = unit
            return lax.dot_general(
                rows_of[at][low : low + each],
                key,
                (((1,), (1,)), ((), ())),
                preferred_element_type=jnp.float32,
            )

        scores = [score(units[0], key) for key in keys[0]]
        for number, (at, low) in enumerate(units):
            here = slice(low, low + each)
            peak = None
            for part in scores:
                for lane in range(0, part.shape[1], head_dim):
                    piece = part[:, lane : lane + head_dim]
                    peak = piece if peak is None else jnp.maximum(peak, piece)
            peak = peak.max(axis=1, keepdims=True)
            if not first:
                before = jnp.concatenate([ref[at, 0] for ref in before_refs], axis=0)[here]
                old_peak = before[:, at_peak:]
                peak = jnp.maximum(peak, old_peak)
            offset = peak * to_exp2
            following = units[number + 1] if number + 1 < len(units) else None
            todo = list(keys[following[0]]) if following else []
            summed = None
            ahead = []
            for value, part in zip(values[at], scores):
                if todo:
                    ahead.append(score(following, todo.pop(0)))
                weight = jnp.exp2(part * to_exp2 - offset).astype(jnp.bfloat16)
                term = jnp.dot(weight, value, preferred_element_type=jnp.float32)
                summed = term if summed is None else summed + term
            if not first:
                fade = jnp.exp2(old_peak * to_exp2 - offset)
                summed = summed + before * fade
            if last:
                out = summed[:, :head_dim] / summed[:, head_dim : head_dim + 1]
                out = out.astype(out_ref.dtype)
                piece = out_ref.shape[3]
                size = min(piece, each)
                for row in range(0, each, size):
                    place, to = divmod(low + row, piece)
                    place = scalar_ref[1 + place]
                    out_ref[place, at, 0, to : to + size] = out[row : row + size]
            else:
                out_ref[at, 0, here, :] = summed
                out_ref[at, 0, here, at_peak:] = peak
            scores = ahead

    pairs = columns // 2
    low_span, high_span = (0, 2), (columns - 2, 2)
    if pairs == 1:
        cases = [(None, [low_span, high_span])]
    else:
        inner = [(2 * pair - 1, 3), (2 * pair, 3)]
        cases = [
            (pair == 0, [low_span, (0, 3)]),
            (pair == pairs - 1, [(columns - 3, 3), high_span]),
        ]
        if pairs > 2:
            cases.append(((pair > 0) & (pair < pairs - 1), inner))
    for at_case, spans in cases:
        for rows in (2, 3):
            case = both == (rows == 3)
            if at_case is not None:
                case = at_case & case
            pl.when(case)(functools.partial(block, spans, rows))


def attend(scalars, queries, states, rows, scale, places=0, head=None):
    columns, heads, _, head_dim = queries[0].shape
    tokens = sum(query.shape[2] for query in queries)
    keys = sum(kv.shape[3] for kv in rows) * 10 // 4
    low, count = (0, heads) if head is None else (head, 1)

    def at_head(h, low):
        return h + low if low else h

    def at_slot(h, c, v):
        return (c ^ (v[v.shape[0] - 1] >> 1), at_head(h, low), 0, 0)

    def at_query(h, c, v):
        return (c, at_head(h, low), 0, 0)

    def kv_spec(kv):
        start = low if kv.shape[1] == heads else 0
        return pl.BlockSpec(
            (columns, 1, 2, kv.shape[3], head_dim),
            lambda h, c, v: (0, at_head(h, start), 0, 0, 0),
        )

    if places:
        each = tokens // places
        out_spec = pl.BlockSpec(
            (places, 2, 1, each, head_dim), lambda h, c, v: (0, c, h, 0, 0)
        )
        out_shape = jax.ShapeDtypeStruct((places, columns, count, each, head_dim), jnp.bfloat16)
    else:
        out_spec = pl.BlockSpec((2, 1, tokens, 2 * head_dim), at_query)
        out_shape = jax.ShapeDtypeStruct((columns, heads, tokens, 2 * head_dim), jnp.float32)
    pairs = count * columns * tokens * keys
    arrays = [*queries, *states, *rows]
    in_specs = [
        pl.BlockSpec((2, 1, query.shape[2], head_dim), at_slot) for query in queries
    ]
    in_specs += [
        pl.BlockSpec((2, 1, state.shape[2], 2 * head_dim), at_query) for state in states
    ]
    in_specs += [kv_spec(kv) for kv in rows]
    return pl.pallas_call(
        functools.partial(
            attention_kernel, len(queries), columns, scale, not states, bool(places)
        ),
        grid_spec=pltpu.PrefetchScalarGridSpec(
            num_scalar_prefetch=1,
            grid=(count, columns // 2),
            in_specs=in_specs,
            out_specs=out_spec,
        ),
        out_shape=out_shape,
        cost_estimate=pl.CostEstimate(
            flops=pairs * head_dim * 8, bytes_accessed=pairs * 4, transcendentals=pairs
        ),
        compiler_params=pltpu.CompilerParams(vmem_limit_bytes=LARGE_VMEM if head else SMALL_VMEM),
        name="tile_attention",
    )(scalars, *arrays)


def mix_kernel(final, at_ref, attended_ref, *refs):
    out_ref = refs[-1]
    weight_refs = refs[: -2 if final else -1]
    total = refs[-2][...] if final else 0.0
    places = [(ref, k) for ref in weight_refs for k in range(ref.shape[0])]
    for at in range(0, len(places), 2):
        pair = places[at : at + 2]
        left = jnp.concatenate([attended_ref[at_ref[at + i]] for i in range(len(pair))], axis=1)
        right = jnp.concatenate(
            [ref[k].reshape(ref.shape[-2:]) for ref, k in pair], axis=0
        )
        total = total + jnp.dot(left, right, preferred_element_type=jnp.float32)
    out_ref[...] = total.astype(out_ref.dtype)


def mix(order, attended, local, head, weights, total, final):
    _, tokens, head_dim = attended.shape
    width = local.shape[-1]
    step = math.gcd(width, 1024)
    heads = local.shape[0] + len(weights)
    out_spec = pl.BlockSpec((tokens, step), lambda i, o: (0, i))
    final_args = [total] if final else []
    return pl.pallas_call(
        functools.partial(mix_kernel, final),
        grid_spec=pltpu.PrefetchScalarGridSpec(
            num_scalar_prefetch=1,
            grid=(width // step,),
            in_specs=[
                pl.BlockSpec(attended.shape, lambda i, o: (0, 0, 0)),
                pl.BlockSpec((local.shape[0], 1, head_dim, step), lambda i, o: (0, head, 0, i)),
            ]
            + [pl.BlockSpec((1, head_dim, step), lambda i, o: (0, 0, i)) for _ in weights]
            + [out_spec for _ in final_args],
            out_specs=out_spec,
        ),
        out_shape=jax.ShapeDtypeStruct((tokens, width), jnp.bfloat16 if final else jnp.float32),
        cost_estimate=pl.CostEstimate(
            flops=2 * heads * tokens * head_dim * width,
            bytes_accessed=2 * heads * head_dim * width,
            transcendentals=0,
        ),
        compiler_params=pltpu.CompilerParams(vmem_limit_bytes=MIX_VMEM),
        name="mix_heads",
    )(order, attended, local, *weights, *final_args)


def row_plan(latents, input_weight, norm_gains, output_weight):
    frame_parts = lax.axis_size("ta")
    row_parts = lax.axis_size("ha")
    col_parts = lax.axis_size("wa")
    heads_local, head_dim = input_weight.shape[2:]
    heads_each = heads_local // col_parts
    here, column_at = lax.axis_index("ta"), lax.axis_index("wa")
    chunks = [latents]
    for by in range(1, frame_parts):
        chunks.append(lax.ppermute(latents, "ta", shift_perm(frame_parts, by)))

    fetched = []
    for by in range(1, frame_parts):
        for mask in range(0, col_parts, 2):
            for k in range(heads_each):
                if mask and (mask, k) == (col_parts - 2, heads_each - 1):
                    continue
                head = (column_at ^ mask) * heads_each + k
                share = lax.dynamic_slice_in_dim(output_weight, head, 1, axis=0)
                share = lax.ppermute(share, "ta", shift_perm(frame_parts, by))
                fetched.append((by, mask, k, share))

    for by, mask, k, share in list(fetched):
        if col_parts > 2 and (mask, k) == (0, heads_each - 1):
            mask = col_parts - 2
            share = lax.ppermute(share, "wa", [(i, i ^ mask) for i in range(col_parts)])
            fetched.append((by, mask, k, share))

    def project(chunk):
        return jnp.einsum(
            "cfhwd,dsne->cfhwsne", chunk, input_weight, preferred_element_type=jnp.float32
        )

    def as_query(projected):
        query = rms_norm(projected, norm_gains[0]).astype(jnp.bfloat16)
        query = query.transpose(4, 0, 1, 2, 3, 5)
        return query.reshape(col_parts, heads_each, -1, head_dim)

    def as_key_value(projected):
        key = rms_norm(projected[:, :, :, :, 0], norm_gains[1]).astype(jnp.bfloat16)
        value = projected[:, :, :, :, 1].astype(jnp.bfloat16)
        halves = [
            half.transpose(4, 0, 1, 2, 3, 5).reshape(col_parts, heads_each, 1, -1, head_dim)
            for half in (key, value)
        ]
        return jnp.concatenate(halves, axis=2)

    queries, keys_values = [], []
    ready = None
    for chunk in chunks:
        if ready is not None:
            chunk = after(chunk, ready)
        projected = project(chunk)
        key_value = as_key_value(projected[:, :, :, :, 1:])
        query = as_query(projected[:, :, :, :, 0])
        ready = (query, key_value)
        dealt = lax.all_to_all(key_value, "wa", 0, 0)
        keys_values.append(after(dealt, query))
        slots = [lax.dynamic_index_in_dim(query, column_at, 0, keepdims=False)]
        for by in range(1, col_parts):
            block = lax.dynamic_index_in_dim(query, column_at ^ by, 0, keepdims=False)
            slots.append(lax.ppermute(block, "wa", [(i, i ^ by) for i in range(col_parts)]))
        queries.append(jnp.stack(slots))
    pair = [(i, i ^ 1) for i in range(row_parts)]
    side = []
    for i in range(row_parts):
        for k in range(col_parts):
            if 0 < i < row_parts - 1:
                to = (((i + 1) ^ 1) - 1) * col_parts + k
            else:
                to = i * col_parts + (k ^ 1)
            side.append((i * col_parts + k, to))
    rows = []
    for at, key_value in enumerate(keys_values):
        shares = [key_value]
        if at:
            shares = [key_value[:, head : head + 1] for head in range(heads_each)]
        paired, beside = [], []
        for head, share in enumerate(shares):
            paired.append(lax.ppermute(share, "ha", pair))
            beside.append(lax.ppermute(share, ("ha", "wa"), side))
        rows.append((key_value, paired, beside))
    height_index = lax.axis_index("ha")
    inside = (height_index > 0) & (height_index < row_parts - 1)
    places = [lax.rem(here + (frame_parts - by), frame_parts) for by in range(frame_parts)]
    scalars = jnp.stack([inside.astype(jnp.int32)] + places + [column_at])
    scale = 1.0 / math.sqrt(head_dim)

    first_rows = [rows[0][0], *rows[0][1], *rows[0][2]]
    states = []
    for query in queries:
        states.append(attend(scalars, [query], [], first_rows, scale))

    swap = [(i, i ^ 1) for i in range(col_parts)]
    spread = []
    for by, mask, k, share in fetched:
        other = lax.ppermute(share, "wa", swap)
        spread.append((by, mask, k, share))
        spread.append((by, mask ^ 1, k, other))
    local = output_weight.reshape(col_parts, heads_each, head_dim, -1)
    total = None
    for head in range(heads_each):
        last_rows = [row[0] for row in rows[1:]]
        last_rows += [row[1][head] for row in rows[1:]] + [row[2][head] for row in rows[1:]]
        attended = attend(scalars, queries, states, last_rows, scale, frame_parts, head)
        sent = attended.reshape(frame_parts * col_parts, -1, head_dim)
        got = lax.all_to_all(sent, ("ta", "wa"), 0, 0, tiled=True)
        got = got.reshape(frame_parts * col_parts, -1, head_dim)
        order = [here * col_parts + k for k in range(col_parts)]
        weights = []
        for by, mask, k, part in spread:
            if k == head:
                weights.append(part)
                order.append(places[by] * col_parts + (column_at ^ mask))
        order = jnp.stack(order).astype(jnp.int32)
        total = mix(order, got, local, head, weights, total, head == heads_each - 1)
    return total.reshape(latents.shape)


def solution(mesh):
    in_specs = (
        P(None, "ta", "ha", "wa", None),
        P(None, None, "ta", None),
        P(),
        P("ta", None, None),
    )
    out_specs = P(None, "ta", "ha", "wa", None)

    def per_device(latents, input_weight, norm_gains, output_weight):
        frames = latents.shape[1] * lax.axis_size("ta")
        width = lax.axis_size("wa")
        dealt_heads = input_weight.shape[2] % width == 0 and width & (width - 1) == 0
        dealt_heads &= lax.axis_size("ha") % 2 == 0 and lax.axis_size("ta") > 1 and width > 1
        if latents.shape[0] == 1 and dealt_heads and frames <= 2 * TILE_T:
            return row_plan(latents, input_weight, norm_gains, output_weight)
        return halo_plan(latents, input_weight, norm_gains, output_weight)

    return jax.shard_map(
        per_device, mesh=mesh, in_specs=in_specs, out_specs=out_specs, check_vma=False
    )
```

```python
import functools
import math

import jax
import jax.numpy as jnp
from jax import lax
from jax.experimental import pallas as pl
from jax.experimental.pallas import tpu as pltpu
from jax.sharding import PartitionSpec as P


TILE_T = 4


EPSILON = 1e-06


def padded(cells, sides, width):
    for axis, dim in sides:
        count = lax.axis_size(axis)
        ends = count - 1
        head = lax.slice_in_dim(cells, 0, width, axis=dim)
        tail = lax.slice_in_dim(cells, cells.shape[dim] - width, cells.shape[dim], axis=dim)
        cells = jnp.concatenate(
            [
                lax.ppermute(tail, axis, [(i, (i + 1) % count) for i in range(ends)]),
                cells,
                lax.ppermute(head, axis, [((i + 1) % count, i) for i in range(ends)]),
            ],
            axis=dim,
        )
    return cells


def rms_norm(values, gain_row):
    mean_square = jnp.mean(values * values, axis=-1, keepdims=True)
    return values * lax.rsqrt(mean_square + EPSILON) * gain_row


def halo_plan(latents, input_weight, norm_gains, output_weight):
    clip_count = latents.shape[0]
    frames_local = latents.shape[1]
    tile_side = latents.shape[2]
    model_width = latents.shape[4]
    heads_local = input_weight.shape[2]
    head_dim = input_weight.shape[3]
    projected = jnp.einsum(
        "cfhwd,dsne->cfhwsne",
        lax.all_gather(latents, "ta", axis=1, tiled=True),
        input_weight,
        preferred_element_type=jnp.float32,
    )
    query_normed = rms_norm(projected[:, :, :, :, 0], norm_gains[0])
    key_normed = rms_norm(projected[:, :, :, :, 1], norm_gains[1])
    stacked = jnp.stack([query_normed, key_normed, projected[:, :, :, :, 2]], axis=4).astype(
        jnp.bfloat16
    )
    frames = stacked.shape[1]
    query_all = stacked[:, :, :, :, 0]
    key_value = stacked[:, :, :, :, 1:]
    beside_all = padded(key_value, (("ha", 2), ("wa", 3)), tile_side)
    height_index = lax.axis_index("ha")
    width_index = lax.axis_index("wa")
    band_rows = jnp.stack(
        [height_index > 0, height_index >= 0, height_index < lax.axis_size("ha") - 1]
    )
    band_cols = jnp.stack(
        [width_index > 0, width_index >= 0, width_index < lax.axis_size("wa") - 1]
    )
    rows_valid = jnp.repeat(band_rows, tile_side)
    cols_valid = jnp.repeat(band_cols, tile_side)
    around_mask = (rows_valid[:, None] & cols_valid[None, :]).reshape(-1)
    spatial = tile_side * tile_side
    around_len = 9 * spatial
    queries = query_all.reshape(clip_count, frames, spatial, heads_local, head_dim)
    keys_all = beside_all[:, :, :, :, 0].reshape(
        clip_count, frames, around_len, heads_local, head_dim
    )
    values_all = beside_all[:, :, :, :, 1].reshape(
        clip_count, frames, around_len, heads_local, head_dim
    )
    inv_root = 1.0 / math.sqrt(head_dim)
    tile_count = -(-frames // TILE_T)
    pieces = []
    for tile_at in range(tile_count):
        query_low = tile_at * TILE_T
        query_high = min(query_low + TILE_T, frames)
        key_low = max(query_low - TILE_T, 0)
        key_high = min(query_low + 2 * TILE_T, frames)
        query_block = queries[:, query_low:query_high].reshape(
            clip_count, (query_high - query_low) * spatial, heads_local, head_dim
        )
        key_block = keys_all.reshape(
            clip_count, (key_high - key_low) * around_len, heads_local, head_dim
        )
        value_block = values_all.reshape(
            clip_count, (key_high - key_low) * around_len, heads_local, head_dim
        )
        key_mask = jnp.tile(around_mask, key_high - key_low)
        scores = (
            jnp.einsum(
                "cqnd,cknd->ncqk", query_block, key_block, preferred_element_type=jnp.float32
            )
            * inv_root
        )
        scores = jnp.where(key_mask, scores, -1e30)
        row_peak = jnp.max(scores, axis=-1, keepdims=True)
        weights = jnp.exp(scores - row_peak)
        probability = (weights / jnp.sum(weights, axis=-1, keepdims=True)).astype(jnp.bfloat16)
        pieces.append(
            jnp.einsum(
                "ncqk,cknd->ncqd", probability, value_block, preferred_element_type=jnp.float32
            ).astype(jnp.bfloat16)
        )
    attended = jnp.concatenate(pieces, axis=2).reshape(
        heads_local, clip_count, frames, spatial, head_dim
    )
    own_rows = lax.psum_scatter(
        jnp.einsum("ncfqd,nde->fcqe", attended, output_weight, preferred_element_type=jnp.float32),
        "ta",
        scatter_dimension=0,
        tiled=True,
    )
    result = own_rows.transpose(1, 0, 2, 3).reshape(
        clip_count, frames_local, tile_side, tile_side, model_width
    )
    return result.astype(jnp.bfloat16)


UNIT_ROWS = 256
SMALL_VMEM = 32 << 20
LARGE_VMEM = 60 << 20
MIX_VMEM = 44 << 20


def shift_perm(count, by):
    return [(i, (i + by) % count) for i in range(count)]


def after(value, earlier):
    return lax.optimization_barrier((value, earlier))[0]


def attention_kernel(parts, columns, scale, first, last, scalar_ref, *refs):
    queries = refs[:parts]
    rest = refs[parts:]
    if not first:
        before_refs, rest = rest[:parts], rest[parts:]
    kv_refs, out_ref = rest[:-1], rest[-1]
    groups = len(kv_refs) // 3
    head_dim = queries[0].shape[-1]
    total_rows = sum(ref.shape[2] for ref in queries)
    each = math.gcd(total_rows, UNIT_ROWS)
    at_peak = 2 * head_dim - 1
    to_exp2 = scale * math.log2(math.e)
    pair = pl.program_id(1)
    both = scalar_ref[0] > 0
    odd = scalar_ref[scalar_ref.shape[0] - 1] & 1

    def block(spans, rows):
        keys, values, rows_of, places_of = [], [], [], []
        for at, (place, start, width) in enumerate(spans):
            keys.append([])
            values.append([])
            places_of.append(place)
            for ref in kv_refs[: rows * groups]:
                tokens = ref.shape[3]
                key = ref[pl.ds(start, width), 0, 0].reshape(width * tokens, head_dim)
                value = ref[pl.ds(start, width), 0, 1].reshape(width * tokens, head_dim)
                keys[at].append(key)
                values[at].append(jnp.concatenate([value, jnp.ones_like(value)], axis=1))
            rows_of.append(jnp.concatenate([ref[place ^ odd, 0] for ref in queries], axis=0))
        units = [(at, low) for at in range(2) for low in range(0, total_rows, each)]

        def score(unit, key):
            at, low = unit
            return lax.dot_general(
                rows_of[at][low : low + each],
                key,
                (((1,), (1,)), ((), ())),
                preferred_element_type=jnp.float32,
            )

        scores = [score(units[0], key) for key in keys[0]]
        for number, (at, low) in enumerate(units):
            here = slice(low, low + each)
            peak = None
            for part in scores:
                for lane in range(0, part.shape[1], head_dim):
                    piece = part[:, lane : lane + head_dim]
                    peak = piece if peak is None else jnp.maximum(peak, piece)
            peak = peak.max(axis=1, keepdims=True)
            if not first:
                before = jnp.concatenate([ref[places_of[at], 0] for ref in before_refs], axis=0)
                before = before[here]
                old_peak = before[:, at_peak:]
                peak = jnp.maximum(peak, old_peak)
            offset = peak * to_exp2
            following = units[number + 1] if number + 1 < len(units) else None
            todo = list(keys[following[0]]) if following else []
            summed = None
            ahead = []
            for value, part in zip(values[at], scores):
                if todo:
                    ahead.append(score(following, todo.pop(0)))
                weight = jnp.exp2(part * to_exp2 - offset).astype(jnp.bfloat16)
                term = jnp.dot(weight, value, preferred_element_type=jnp.float32)
                summed = term if summed is None else summed + term
            if not first:
                fade = jnp.exp2(old_peak * to_exp2 - offset)
                summed = summed + before * fade
            if last:
                out = summed[:, :head_dim] / summed[:, head_dim : head_dim + 1]
                out = out.astype(out_ref.dtype)
                piece = out_ref.shape[3]
                size = min(piece, each)
                for row in range(0, each, size):
                    place, to = divmod(low + row, piece)
                    place = scalar_ref[1 + place]
                    out_ref[place, places_of[at], 0, to : to + size] = out[row : row + size]
            else:
                out_ref[places_of[at], 0, here, :] = summed
                out_ref[places_of[at], 0, here, at_peak:] = peak
            scores = ahead

    pairs = columns // 2
    low_end = pair == 0
    outer = jnp.where(low_end, 0, 1)
    outer_span = (outer, jnp.where(low_end, 0, columns - 2), 2)
    if pairs == 1:
        cases = [(None, [(0, 0, 2), (1, 0, 2)])]
    else:
        at_end = low_end | (pair == pairs - 1)
        cases = [(at_end, [outer_span, (1 - outer, jnp.where(low_end, 0, columns - 3), 3)])]
        if pairs > 2:
            inner = [(0, 2 * pair - 1, 3), (1, 2 * pair, 3)]
            cases.append((jnp.logical_not(at_end), inner))
        else:
            cases = [(None, cases[0][1])]
    for at_case, spans in cases:
        for rows in (2, 3):
            case = both == (rows == 3)
            if at_case is not None:
                case = at_case & case
            pl.when(case)(functools.partial(block, spans, rows))


def attend(scalars, queries, states, rows, scale, places=0, head=None):
    columns, heads, _, head_dim = queries[0].shape
    tokens = sum(query.shape[2] for query in queries)
    keys = sum(kv.shape[3] for kv in rows) * 10 // 4
    low, count = (0, heads) if head is None else (head, 1)

    def at_head(h, low):
        return h + low if low else h

    def at_slot(h, c, v):
        return (c ^ (v[v.shape[0] - 1] >> 1), at_head(h, low), 0, 0)

    def at_query(h, c, v):
        return (c, at_head(h, low), 0, 0)

    def kv_spec(kv):
        start = low if kv.shape[1] == heads else 0
        return pl.BlockSpec(
            (columns, 1, 2, kv.shape[3], head_dim),
            lambda h, c, v: (0, at_head(h, start), 0, 0, 0),
        )

    if places:
        each = tokens // places
        out_spec = pl.BlockSpec(
            (places, 2, 1, each, head_dim), lambda h, c, v: (0, c, h, 0, 0)
        )
        out_shape = jax.ShapeDtypeStruct((places, columns, count, each, head_dim), jnp.bfloat16)
    else:
        out_spec = pl.BlockSpec((2, 1, tokens, 2 * head_dim), at_query)
        out_shape = jax.ShapeDtypeStruct((columns, heads, tokens, 2 * head_dim), jnp.float32)
    pairs = count * columns * tokens * keys
    arrays = [*queries, *states, *rows]
    in_specs = [
        pl.BlockSpec((2, 1, query.shape[2], head_dim), at_slot) for query in queries
    ]
    in_specs += [
        pl.BlockSpec((2, 1, state.shape[2], 2 * head_dim), at_query) for state in states
    ]
    in_specs += [kv_spec(kv) for kv in rows]
    return pl.pallas_call(
        functools.partial(
            attention_kernel, len(queries), columns, scale, not states, bool(places)
        ),
        grid_spec=pltpu.PrefetchScalarGridSpec(
            num_scalar_prefetch=1,
            grid=(count, columns // 2),
            in_specs=in_specs,
            out_specs=out_spec,
        ),
        out_shape=out_shape,
        cost_estimate=pl.CostEstimate(
            flops=pairs * head_dim * 8, bytes_accessed=pairs * 4, transcendentals=pairs
        ),
        compiler_params=pltpu.CompilerParams(vmem_limit_bytes=LARGE_VMEM if head else SMALL_VMEM),
        name="tile_attention",
    )(scalars, *arrays)


def mix_kernel(final, at_ref, attended_ref, *refs):
    out_ref = refs[-1]
    weight_refs = refs[: -2 if final else -1]
    total = refs[-2][...] if final else 0.0
    places = [(ref, k) for ref in weight_refs for k in range(ref.shape[0])]
    for at in range(0, len(places), 2):
        pair = places[at : at + 2]
        left = jnp.concatenate([attended_ref[at_ref[at + i]] for i in range(len(pair))], axis=1)
        right = jnp.concatenate(
            [ref[k].reshape(ref.shape[-2:]) for ref, k in pair], axis=0
        )
        total = total + jnp.dot(left, right, preferred_element_type=jnp.float32)
    out_ref[...] = total.astype(out_ref.dtype)


def mix(order, attended, local, head, weights, total, final):
    _, tokens, head_dim = attended.shape
    width = local.shape[-1]
    step = math.gcd(width, 1024)
    heads = local.shape[0] + len(weights)
    out_spec = pl.BlockSpec((tokens, step), lambda i, o: (0, i))
    final_args = [total] if final else []
    return pl.pallas_call(
        functools.partial(mix_kernel, final),
        grid_spec=pltpu.PrefetchScalarGridSpec(
            num_scalar_prefetch=1,
            grid=(width // step,),
            in_specs=[
                pl.BlockSpec(attended.shape, lambda i, o: (0, 0, 0)),
                pl.BlockSpec((local.shape[0], 1, head_dim, step), lambda i, o: (0, head, 0, i)),
            ]
            + [pl.BlockSpec((1, head_dim, step), lambda i, o: (0, 0, i)) for _ in weights]
            + [out_spec for _ in final_args],
            out_specs=out_spec,
        ),
        out_shape=jax.ShapeDtypeStruct((tokens, width), jnp.bfloat16 if final else jnp.float32),
        cost_estimate=pl.CostEstimate(
            flops=2 * heads * tokens * head_dim * width,
            bytes_accessed=2 * heads * head_dim * width,
            transcendentals=0,
        ),
        compiler_params=pltpu.CompilerParams(vmem_limit_bytes=MIX_VMEM),
        name="mix_heads",
    )(order, attended, local, *weights, *final_args)


def row_plan(latents, input_weight, norm_gains, output_weight):
    frame_parts = lax.axis_size("ta")
    row_parts = lax.axis_size("ha")
    col_parts = lax.axis_size("wa")
    heads_local, head_dim = input_weight.shape[2:]
    heads_each = heads_local // col_parts
    here, column_at = lax.axis_index("ta"), lax.axis_index("wa")
    chunks = [latents]
    for by in range(1, frame_parts):
        chunks.append(lax.ppermute(latents, "ta", shift_perm(frame_parts, by)))

    fetched = []
    for by in range(1, frame_parts):
        for mask in range(0, col_parts, 2):
            for k in range(heads_each):
                if mask and (mask, k) == (col_parts - 2, heads_each - 1):
                    continue
                head = (column_at ^ mask) * heads_each + k
                share = lax.dynamic_slice_in_dim(output_weight, head, 1, axis=0)
                share = lax.ppermute(share, "ta", shift_perm(frame_parts, by))
                fetched.append((by, mask, k, share))

    for by, mask, k, share in list(fetched):
        if col_parts > 2 and (mask, k) == (0, heads_each - 1):
            mask = col_parts - 2
            share = lax.ppermute(share, "wa", [(i, i ^ mask) for i in range(col_parts)])
            fetched.append((by, mask, k, share))

    def project(chunk):
        return jnp.einsum(
            "cfhwd,dsne->cfhwsne", chunk, input_weight, preferred_element_type=jnp.float32
        )

    def as_query(projected):
        query = rms_norm(projected, norm_gains[0]).astype(jnp.bfloat16)
        query = query.transpose(4, 0, 1, 2, 3, 5)
        return query.reshape(col_parts, heads_each, -1, head_dim)

    def as_key_value(projected):
        key = rms_norm(projected[:, :, :, :, 0], norm_gains[1]).astype(jnp.bfloat16)
        value = projected[:, :, :, :, 1].astype(jnp.bfloat16)
        halves = [
            half.transpose(4, 0, 1, 2, 3, 5).reshape(col_parts, heads_each, 1, -1, head_dim)
            for half in (key, value)
        ]
        return jnp.concatenate(halves, axis=2)

    queries, keys_values = [], []
    ready = None
    for chunk in chunks:
        if ready is not None:
            chunk = after(chunk, ready)
        projected = project(chunk)
        key_value = as_key_value(projected[:, :, :, :, 1:])
        query = as_query(projected[:, :, :, :, 0])
        ready = (query, key_value)
        dealt = lax.all_to_all(key_value, "wa", 0, 0)
        keys_values.append(after(dealt, query))
        slots = [lax.dynamic_index_in_dim(query, column_at, 0, keepdims=False)]
        for by in range(1, col_parts):
            block = lax.dynamic_index_in_dim(query, column_at ^ by, 0, keepdims=False)
            slots.append(lax.ppermute(block, "wa", [(i, i ^ by) for i in range(col_parts)]))
        queries.append(jnp.stack(slots))
    pair = [(i, i ^ 1) for i in range(row_parts)]
    side = []
    for i in range(row_parts):
        for k in range(col_parts):
            if 0 < i < row_parts - 1:
                to = (((i + 1) ^ 1) - 1) * col_parts + k
            else:
                to = i * col_parts + (k ^ 1)
            side.append((i * col_parts + k, to))
    rows = []
    for at, key_value in enumerate(keys_values):
        shares = [key_value]
        if at:
            shares = [key_value[:, head : head + 1] for head in range(heads_each)]
        paired, beside = [], []
        for head, share in enumerate(shares):
            paired.append(lax.ppermute(share, "ha", pair))
            beside.append(lax.ppermute(share, ("ha", "wa"), side))
        rows.append((key_value, paired, beside))
    height_index = lax.axis_index("ha")
    inside = (height_index > 0) & (height_index < row_parts - 1)
    places = [lax.rem(here + (frame_parts - by), frame_parts) for by in range(frame_parts)]
    scalars = jnp.stack([inside.astype(jnp.int32)] + places + [column_at])
    scale = 1.0 / math.sqrt(head_dim)

    first_rows = [rows[0][0], *rows[0][1], *rows[0][2]]
    states = []
    for query in queries:
        states.append(attend(scalars, [query], [], first_rows, scale))

    swap = [(i, i ^ 1) for i in range(col_parts)]
    spread = []
    for by, mask, k, share in fetched:
        other = lax.ppermute(share, "wa", swap)
        spread.append((by, mask, k, share))
        spread.append((by, mask ^ 1, k, other))
    local = output_weight.reshape(col_parts, heads_each, head_dim, -1)
    total = None
    for head in range(heads_each):
        last_rows = [row[0] for row in rows[1:]]
        last_rows += [row[1][head] for row in rows[1:]] + [row[2][head] for row in rows[1:]]
        attended = attend(scalars, queries, states, last_rows, scale, frame_parts, head)
        sent = attended.reshape(frame_parts * col_parts, -1, head_dim)
        got = lax.all_to_all(sent, ("ta", "wa"), 0, 0, tiled=True)
        got = got.reshape(frame_parts * col_parts, -1, head_dim)
        order = [here * col_parts + k for k in range(col_parts)]
        weights = []
        for by, mask, k, part in spread:
            if k == head:
                weights.append(part)
                order.append(places[by] * col_parts + (column_at ^ mask))
        order = jnp.stack(order).astype(jnp.int32)
        total = mix(order, got, local, head, weights, total, head == heads_each - 1)
    return total.reshape(latents.shape)


def solution(mesh):
    in_specs = (
        P(None, "ta", "ha", "wa", None),
        P(None, None, "ta", None),
        P(),
        P("ta", None, None),
    )
    out_specs = P(None, "ta", "ha", "wa", None)

    def per_device(latents, input_weight, norm_gains, output_weight):
        frames = latents.shape[1] * lax.axis_size("ta")
        width = lax.axis_size("wa")
        dealt_heads = input_weight.shape[2] % width == 0 and width & (width - 1) == 0
        dealt_heads &= lax.axis_size("ha") % 2 == 0 and lax.axis_size("ta") > 1 and width > 1
        if latents.shape[0] == 1 and dealt_heads and frames <= 2 * TILE_T:
            return row_plan(latents, input_weight, norm_gains, output_weight)
        return halo_plan(latents, input_weight, norm_gains, output_weight)

    return jax.shard_map(
        per_device, mesh=mesh, in_specs=in_specs, out_specs=out_specs, check_vma=False
    )
```
